32 devices in a mesh: src: 4 (over y, x), tgt: 8 (over z, core).
Axes of the slice: x: 2, y: 2, z: 4, core: 2. Of those that a mesh axis runs over, the one named last changes fastest.
Arguments:
- src_codes: bfloat16 [1024, 6144], P('tgt', 'src'), may hold values from -1 to 1
- src_scale: float32 [6144], P('src'), may hold values from 0.8 to 1.25
- tgt_codes: bfloat16 [1024, 8192], P('src', 'tgt'), may hold values from -1 to 1
- tgt_scale: float32 [8192], P('tgt'), may hold values from 0.8 to 1.25
Outputs:
- forward_best: float32 [4, 6144], P(None, 'src')
- backward_best: float32 [4, 8192], P(None, 'tgt')
The draws below stay inside these ranges and needn't reach their ends.
All inputs are finite; a program needn't handle non-finite values.
Results may differ from the reference program's by a relative error of at most 0.0003.
Values may be sent and summed in bfloat16 or wider, within the bound.
No kernel may reach another device: no remote copies, remote signals or barrier semaphores. Data moves between devices by JAX's collectives and lax.ppermute only.
A program may use at most 64 MiB of HBM per device.

```python
import math
import jax
import jax.numpy as jnp
from jax import lax

D = 1024
KNN = 4
KEEP = 4
NS = 6144
NT = 8192


def rough_noise(key, extent):
    return jnp.clip(0.25 * jax.random.normal(key, extent, jnp.float32), -1.0, 1.0)


def unit_noise(key, extent):
    return jnp.clip(jax.random.normal(key, extent, jnp.float32), -2.0, 2.0)


def shared_direction(key):
    return unit_noise(jax.random.fold_in(key, 21), (D,))


def target_groups(key):
    return rough_noise(jax.random.fold_in(key, 11), (D, NT // 4))


def hub_flags(key):
    groups = NT // 4
    slot = jax.random.randint(jax.random.fold_in(key, 22), (groups // 16 + 1,), 0, 16)
    places = jnp.arange(groups, dtype=jnp.int32)
    return jnp.where(places % 16 == jnp.take(slot, places // 16), 1.0, 0.0).astype(jnp.float32)


def draw_tgt_codes(key, part):
    bases = target_groups(key)
    shared = shared_direction(key)
    member = jnp.arange(NT, dtype=jnp.int32) // 4
    copies = 0.04 * unit_noise(jax.random.fold_in(key, 23), (D, NT))
    hubs = jnp.take(hub_flags(key), member)
    columns = jnp.take(bases, member, axis=1) + copies + 0.25 * hubs[None, :] * shared[:, None]
    return jnp.clip(columns, -1.0, 1.0).astype(jnp.bfloat16)


def draw_src_codes(key, part):
    groups = NS // 4
    bases = target_groups(key)
    shared = shared_direction(key)
    partner = jax.random.randint(jax.random.fold_in(key, 12), (groups,), 0, NT // 4)
    paired = jax.random.randint(jax.random.fold_in(key, 13), (groups,), 0, 2)
    strength = jax.random.uniform(jax.random.fold_in(key, 14), (groups,), jnp.float32, 0.45, 0.85)
    strong = jax.random.randint(jax.random.fold_in(key, 24), (groups,), 0, 32)
    weight = jnp.where(strong == 0, 0.3, 0.05).astype(jnp.float32)
    source_noise = rough_noise(jax.random.fold_in(key, 15), (D, groups))
    blended = strength[None, :] * jnp.take(bases, partner, axis=1) + jnp.sqrt(1.0 - strength * strength)[None, :] * source_noise
    chosen = jnp.where(paired[None, :] == 1, blended, source_noise)
    member = jnp.arange(NS, dtype=jnp.int32) // 4
    copies = 0.04 * unit_noise(jax.random.fold_in(key, 25), (D, NS))
    columns = jnp.take(chosen, member, axis=1) + copies + jnp.take(weight, member)[None, :] * shared[:, None]
    return jnp.clip(columns, -1.0, 1.0).astype(jnp.bfloat16)


def levels(own_key, shape, pieces, least, top_value):
    def one(position, blocks):
        heights = jax.random.uniform(jax.random.fold_in(jax.random.fold_in(own_key, 6), position), (blocks,), jnp.float32, least / len(pieces), top_value / len(pieces))
        return jnp.repeat(jnp.exp(heights), shape[position] // blocks).reshape((-1,) + (1,) * (len(shape) - position - 1))

    gain = one(*pieces[0])
    for cut in pieces[1:]:
        gain = gain * one(*cut)
    return gain


def setup_inputs(seed: int = 0) -> dict:
    key_list = jax.random.split(jax.random.key(seed), 5)
    return {
        "src_codes": draw_src_codes(jax.random.fold_in(key_list[4], 71), 0),
        "src_scale": jnp.clip(jnp.exp(math.log(1.25) - 0.4462871 * jax.random.uniform(key_list[1], (NS,), jnp.float32) ** levels(key_list[1], (NS,), ((0, 4),), -0.2, 0.2)), 0.8, 1.25),
        "tgt_codes": draw_tgt_codes(jax.random.fold_in(key_list[4], 71), 0),
        "tgt_scale": jnp.clip(jnp.exp(math.log(1.25) - 0.4462871 * jax.random.uniform(key_list[3], (NT,), jnp.float32) ** levels(key_list[3], (NT,), ((0, 8),), -0.2, 0.2)), 0.8, 1.25),
    }


def tile_scores(block, block_scale, targets, target_scale):
    dots = lax.dot_general(block, targets, (((0,), (0,)), ((), ())), preferred_element_type=jnp.float32)
    return dots * block_scale[:, None] * target_scale[None, :]


def merge_lists(first, second):
    return lax.top_k(jnp.concatenate([first, second], axis=1), first.shape[1])[0]


def sweep(sources, source_scale, targets, target_scale, source_denom, target_denom, use_margin, width):
    rows = sources.shape[1]
    step = 512 if rows % 512 == 0 else rows
    count = rows // step
    items = (jnp.arange(count, dtype=jnp.int32), source_scale.reshape(count, step), source_denom.reshape(count, step))

    def visit(carry, item):
        index, scale, denom = item
        block = lax.dynamic_slice_in_dim(sources, (index * step).astype(jnp.int32), step, 1)
        sim = tile_scores(block, scale, targets, target_scale)
        if use_margin:
            sim = sim / (0.5 * (denom[:, None] + target_denom[None, :]))
        ahead = lax.top_k(sim, width)[0]
        column = lax.top_k(sim.T, width)[0]
        return merge_lists(carry, column), ahead

    start = jnp.full((targets.shape[1], width), -1e30, jnp.float32)
    behind, ahead = lax.scan(visit, start, items)
    return ahead.reshape(rows, width), behind


def reference(src_codes, src_scale, tgt_codes, tgt_scale):
    dummy_src = jnp.ones_like(src_scale)
    dummy_tgt = jnp.ones_like(tgt_scale)
    ahead, behind = sweep(src_codes, src_scale, tgt_codes, tgt_scale, dummy_src, dummy_tgt, False, KNN)
    forward_knn = jnp.mean(ahead, axis=1)
    backward_knn = jnp.mean(behind, axis=1)
    best_ahead, best_behind = sweep(src_codes, src_scale, tgt_codes, tgt_scale, forward_knn, backward_knn, True, KEEP)
    return best_ahead.T, best_behind.T
```

```python
import functools

import jax
import jax.numpy as jnp
from jax import lax
from jax.experimental import pallas as pl
from jax.experimental.pallas import tpu as pltpu
from jax.sharding import PartitionSpec as P

TOP = 4
LANES = 128
GROUP = 512
ANY = pl.BlockSpec(memory_space=pl.ANY)
VMEM = pl.BlockSpec(memory_space=pltpu.VMEM)


def params():
    return pltpu.CompilerParams(vmem_limit_bytes=20 << 20)


def exchange(a, b):
    return jnp.maximum(a, b), jnp.minimum(a, b)


def sort4(v):
    a, b, c, d = v
    a, b = exchange(a, b)
    c, d = exchange(c, d)
    a, c = exchange(a, c)
    b, d = exchange(b, d)
    b, c = exchange(b, c)
    return [a, b, c, d]


def merge4(p, q):
    m = [jnp.maximum(p[k], q[TOP - 1 - k]) for k in range(TOP)]
    m[0], m[2] = exchange(m[0], m[2])
    m[1], m[3] = exchange(m[1], m[3])
    m[0], m[1] = exchange(m[0], m[1])
    m[2], m[3] = exchange(m[2], m[3])
    return m


def over_sublanes(lists):
    for shift in (4, 2, 1):
        lists = merge4(lists, [pltpu.roll(x, shift, 0) for x in lists])
    return lists


def sweep_columns(tile, group, rows, first, fwd_write, state):
    def body(r, lists):
        lists = [list(lists[4 * b : 4 * b + 4]) for b in range(4)]
        v = [[tile(group, r, a, b) for b in range(4)] for a in range(4)]
        for b in range(4):
            lists[b] = merge4(lists[b], sort4([v[a][b] for a in range(4)]))
        for a in range(4):
            s = sort4(v[a])
            at = pl.ds(r * 32 + 8 * a, 8)
            if not first:
                s = merge4(s, [state[k, at, :] for k in range(TOP)])
            for k in range(TOP):
                state[k, at, :] = s[k]
        return tuple(x for group_lists in lists for x in group_lists)

    empty = tuple(jnp.full((8, LANES), -jnp.inf, jnp.float32) for _ in range(16))
    lists = lax.fori_loop(0, rows // 32, body, empty)
    for b in range(4):
        best = over_sublanes(list(lists[4 * b : 4 * b + 4]))
        for k in range(TOP):
            fwd_write(k, group * 4 + b, best[k][0:1, :])


def finish_rows(rows, write, state):
    def body(c, _):
        x = [state[k, pl.ds(c * LANES, LANES), :].T for k in range(TOP)]
        lists = [[x[k][8 * g : 8 * g + 8, :] for k in range(TOP)] for g in range(LANES // 8)]
        while len(lists) > 1:
            lists = [merge4(lists[i], lists[i + 1]) for i in range(0, len(lists), 2)]
        best = over_sublanes(lists[0])
        for k in range(TOP):
            write(k, c, best[k][0:1, :])
        return 0

    lax.fori_loop(0, rows // LANES, body, 0)


def column_of(row):
    return jnp.broadcast_to(row, (LANES, LANES)).T


def pack_roles(core, fwd, bwd, send, keep):
    sources, targets = fwd.shape[1], bwd.shape[1]

    @pl.when(core == 0)
    def _():
        send[...] = jnp.zeros_like(send)
        keep[...] = jnp.zeros_like(keep)
        send[:, :targets, :] = bwd[...]
        keep[:, :sources, :] = fwd[...]

    @pl.when(core == 1)
    def _():
        send[...] = jnp.zeros_like(send)
        keep[...] = jnp.zeros_like(keep)
        send[:, :sources, :] = fwd[...]
        keep[:, targets : 2 * targets, :] = bwd[...]


def score_kernel(plan, *refs):
    (masks, last, depth, offset, nsrc, ntgt) = plan
    npieces = 1 + 2 * (depth - 1)
    src = refs[:npieces]
    tgt = refs[npieces : npieces + ntgt]
    rest = refs[npieces + ntgt :]
    if last:
        (scale_s, scale_t, fwd_in, state_in, sim, send, keep,
         src_buf, tgt_buf, column, lane, state, fwd, bwd, src_sem, tgt_sem, in_sem) = rest
    else:
        (scale_s, scale_t, sim, fwd_out, state_out,
         src_buf, tgt_buf, column, lane, src_sem, tgt_sem) = rest
        state = state_out
    t, s = lax.axis_index("tgt"), lax.axis_index("src")
    core, z = t % 2, t // 2
    rows = src[0].shape[0] // 2
    height = tgt[0].shape[0]
    width, targets = src_buf.shape[1], tgt_buf.shape[1]

    def src_copies(i):
        k = (i + 1) // 2
        mine = i % 2 == 1 or i == 0
        if i == 0:
            block, ok = z, None
        else:
            below = core == (0 if mine else 1)
            block = jnp.where(below, z - k, z + k)
            ok = jnp.logical_and(block >= 0, block < depth)
            block = jnp.clip(block, 0, depth - 1)
        head = core if mine else 1 - core
        out = []
        for half, place in ((0, head), (1, 1 - head)):
            at = pl.multiple_of((block * 2 + place) * rows, rows)
            out.append(pltpu.make_async_copy(
                src[i].at[pl.ds(half * rows, rows), :], src_buf.at[pl.ds(at, rows), :], src_sem.at[i, half]))
        return ok, out

    def each_src(act):
        for i in range(npieces):
            ok, copies = src_copies(i)
            if ok is None:
                for c in copies:
                    act(c)
            else:
                @pl.when(ok)
                def _():
                    for c in copies:
                        act(c)

    def tgt_copy(i):
        at = jnp.where(core == 0, s ^ masks[i][0], s ^ masks[i][1]) * height
        return pltpu.make_async_copy(tgt[i], tgt_buf.at[pl.ds(pl.multiple_of(at, height), height), :], tgt_sem.at[i])

    each_src(lambda c: c.start())
    for i in range(ntgt):
        tgt_copy(i).start()
    if last:
        state_copy = pltpu.make_async_copy(state_in, state, in_sem)
        state_copy.start()
    for c in range(targets // LANES):
        column[pl.ds(c * LANES, LANES), :] = column_of(scale_t[pl.ds(c, 1), :])
    for c in range(width // LANES):
        lane[:, pl.ds(c * LANES, LANES)] = jnp.broadcast_to(
            scale_s[pl.ds(offset // LANES + c, 1), :], (8, LANES))
    each_src(lambda c: c.wait())
    for i in range(ntgt):
        tgt_copy(i).wait()

    block_rows = 256
    for g in range(width // GROUP):
        cols = pl.ds(g * GROUP, GROUP)
        for r in range(targets // block_rows):
            sim[pl.ds(r * block_rows, block_rows), cols] = lax.dot_general(
                tgt_buf[:, pl.ds(r * block_rows, block_rows)], src_buf[:, cols],
                (((0,), (0,)), ((), ())), preferred_element_type=jnp.float32)
    if last:
        state_copy.wait()

    def tile(group, r, a, b):
        at, cols = pl.ds(r * 32 + 8 * a, 8), pl.ds(group * GROUP + LANES * b, LANES)
        v = sim[at, cols] * lane[:, cols] * column[at, :]
        sim[at, cols] = v
        return v

    if last:
        before = fwd_in.shape[1]
        fwd[:, :before, :] = fwd_in[...]

        def write(k, c, row):
            fwd[k, pl.ds(before + c, 1), :] = row
    else:
        def write(k, c, row):
            fwd_out[k, pl.ds(c, 1), :] = row

    for g in range(width // GROUP):
        sweep_columns(tile, g, targets, g == 0 and not last, write, state)
    if last:
        def write_rows(k, c, row):
            bwd[k, pl.ds(c, 1), :] = row

        finish_rows(targets, write_rows, state)
        pack_roles(core, fwd, bwd, send, keep)


def margin_kernel(nsim, *refs):
    sims = refs[:nsim]
    mine, theirs, send, keep, column, lane, state, fwd, bwd = refs[nsim:]
    core = lax.axis_index("tgt") % 2
    targets = sims[0].shape[0]
    nt, ns = targets // LANES, fwd.shape[1]
    zero = core == 0
    b = 0.5 * jnp.where(zero, theirs[:nt, :], mine[nt : 2 * nt, :])
    f = 0.5 * jnp.where(zero, mine[:ns, :], theirs[:ns, :])
    for c in range(nt):
        column[pl.ds(c * LANES, LANES), :] = column_of(b[c : c + 1, :])
    for c in range(ns):
        lane[:, pl.ds(c * LANES, LANES)] = jnp.broadcast_to(f[c : c + 1, :], (8, LANES))
    base = 0
    for i in range(nsim):
        sim = sims[i]

        def tile(group, r, a, b, sim=sim, base=base):
            at, cols = pl.ds(r * 32 + 8 * a, 8), pl.ds(group * GROUP + LANES * b, LANES)
            wide = pl.ds(base + group * GROUP + LANES * b, LANES)
            return sim[at, cols] / (lane[:, wide] + column[at, :])

        def write(k, c, row, base=base):
            fwd[k, pl.ds(base // LANES + c, 1), :] = row

        for g in range(sim.shape[1] // GROUP):
            sweep_columns(tile, g, targets, i == 0 and g == 0, write, state)
        base += sim.shape[1]

    def write_rows(k, c, row):
        bwd[k, pl.ds(c, 1), :] = row

    finish_rows(targets, write_rows, state)
    pack_roles(core, fwd, bwd, send, keep)


def join_kernel(targets, keep, rec, out):
    core = lax.axis_index("tgt") % 2
    merged = merge4([keep[k] for k in range(TOP)], [rec[k] for k in range(TOP)])
    row = lax.broadcasted_iota(jnp.int32, merged[0].shape, 0)
    for k in range(TOP):
        both = jnp.where(row < targets, rec[k], keep[k])
        out[k] = jnp.where(core == 0, merged[k], both)


def merge_kernel(active, average, mine, rec, out):
    core = lax.axis_index("tgt") % 2
    merged = merge4([mine[k] for k in range(TOP)], [rec[k] for k in range(TOP)])
    if active != (True, True):
        use = core == (0 if active[0] else 1)
        merged = [jnp.where(use, merged[k], mine[k]) for k in range(TOP)]
    if average:
        out[...] = 0.25 * (merged[0] + merged[1] + merged[2] + merged[3])
    else:
        for k in range(TOP):
            out[k] = merged[k]


def final_kernel(mine, theirs, forward, backward):
    zero = lax.axis_index("tgt") % 2 == 0
    nt, ns = backward.shape[1] // LANES, forward.shape[1] // LANES
    for k in range(TOP):
        f = jnp.where(zero, mine[k], theirs[k])
        for c in range(ns):
            forward[pl.ds(k, 1), pl.ds(c * LANES, LANES)] = f[c : c + 1, :]
        b = jnp.where(zero, theirs[k, :nt, :], mine[k, nt : 2 * nt, :])
        for c in range(nt):
            backward[pl.ds(k, 1), pl.ds(c * LANES, LANES)] = b[c : c + 1, :]


def f32(*shape):
    return jax.ShapeDtypeStruct(shape, jnp.float32)


def cost(flops, moved):
    return pl.CostEstimate(flops=flops, bytes_accessed=moved, transcendentals=0)


def solution(mesh):
    n_src, n_tgt = mesh.shape["src"], mesh.shape["tgt"]
    depth = n_tgt // 2
    src_bits, z_bits = n_src.bit_length() - 1, depth.bit_length() - 1
    both = ("src", "tgt")

    def flat(s, t):
        return s * n_tgt + t

    devices = [(s, t) for s in range(n_src) for t in range(n_tgt)]
    partner = [(t, t ^ 1) for t in range(n_tgt)]

    def swap(x):
        return lax.ppermute(x, "tgt", partner)

    def along_z(x, step):
        pairs = []
        for t in range(n_tgt):
            z, core = t // 2, t % 2
            if core == 0 and z >= step - 1 and z + 1 < depth:
                pairs.append((t, t + 2))
            if core == 1 and z <= depth - step and z >= 1:
                pairs.append((t, t - 2))
        return lax.ppermute(x, "tgt", pairs)

    def src_masks(step):
        return 1 << step, 1 << (src_bits - 1 - step)

    def along_src(x, masks):
        pairs = [(flat(s, t), flat(s ^ masks[t % 2], t)) for s, t in devices]
        return lax.ppermute(x, both, pairs)

    def reduce_lists(send, keep, average):
        r = keep.shape[1]
        rec = swap(send)
        lists = pl.pallas_call(
            functools.partial(join_kernel, r_targets), out_shape=f32(TOP, r, LANES),
            in_specs=[VMEM] * 2, out_specs=VMEM, name="join")(keep, rec)
        steps = max(src_bits, z_bits)
        for step in range(steps):
            active = (step < z_bits, step < src_bits)
            pairs = []
            for s, t in devices:
                z, core = t // 2, t % 2
                if core == 0 and active[0]:
                    pairs.append((flat(s, t), flat(s, (z ^ (1 << step)) * 2)))
                if core == 1 and active[1]:
                    pairs.append((flat(s, t), flat(s ^ (1 << step), t)))
            rec = lax.ppermute(lists, both, pairs)
            mean = average and step == steps - 1
            lists = pl.pallas_call(
                functools.partial(merge_kernel, active, mean),
                out_shape=f32(r, LANES) if mean else f32(TOP, r, LANES),
                in_specs=[VMEM] * 2, out_specs=VMEM, name="merge")(lists, rec)
        return lists

    def body(src_codes, src_scale, tgt_codes, tgt_scale):
        nonlocal r_targets
        sources, targets = src_codes.shape[1], tgt_codes.shape[1]
        total = src_codes.shape[0] * n_tgt
        r_targets = targets // LANES
        r = max(sources // LANES, 2 * r_targets)
        scale_s, scale_t = src_scale.reshape(-1, LANES), tgt_scale.reshape(-1, LANES)

        cuts = [0, sources - GROUP, sources]
        own = [src_codes[:, a:b] for a, b in zip(cuts, cuts[1:])]
        pairs = [jnp.concatenate([x, swap(x)], axis=0) for x in own]

        held = [(tgt_codes, (0, 0))]
        for step in range(src_bits):
            masks = src_masks(step)
            held += [(along_src(x, masks), (m[0] ^ masks[0], m[1] ^ masks[1])) for x, m in held]
        tgt_pieces, tgt_masks = [x for x, _ in held], [m for _, m in held]

        moving = list(pairs)
        pieces = [[p] for p in pairs]
        for step in range(1, depth):
            for i in range(len(pairs)):
                moving[i] = along_z(moving[i], step)
                pieces[i] += [moving[i], swap(moving[i])]

        sims = []
        fwd = state = None
        for i in range(len(pairs)):
            last = i == len(pairs) - 1
            width = cuts[i + 1] - cuts[i]
            plan = (tgt_masks, last, depth, cuts[i], len(pieces[i]), len(tgt_pieces))
            scratch = [
                pltpu.VMEM((total, width), jnp.bfloat16),
                pltpu.VMEM((total, targets), jnp.bfloat16),
                pltpu.VMEM((targets, LANES), jnp.float32),
                pltpu.VMEM((8, width), jnp.float32),
            ]
            sems = [pltpu.SemaphoreType.DMA((len(pieces[i]), 2)), pltpu.SemaphoreType.DMA((len(tgt_pieces),))]
            args = [*pieces[i], *tgt_pieces, scale_s, scale_t]
            specs = [ANY] * (len(pieces[i]) + len(tgt_pieces)) + [VMEM] * 2
            if last:
                args += [fwd, state]
                specs += [VMEM, ANY]
                out = (f32(targets, width), f32(TOP, r, LANES), f32(TOP, r, LANES))
                scratch += [
                    pltpu.VMEM((TOP, targets, LANES), jnp.float32),
                    pltpu.VMEM((TOP, sources // LANES, LANES), jnp.float32),
                    pltpu.VMEM((TOP, r_targets, LANES), jnp.float32),
                ]
                sems += [pltpu.SemaphoreType.DMA]
            else:
                out = (f32(targets, width), f32(TOP, width // LANES, LANES), f32(TOP, targets, LANES))
            res = pl.pallas_call(
                functools.partial(score_kernel, plan), out_shape=out, in_specs=specs,
                out_specs=(VMEM,) * 3, scratch_shapes=scratch + sems, compiler_params=params(),
                cost_estimate=cost(2 * total * width * targets, 4 * width * targets), name=f"score{i}")(*args)
            sims.append(res[0])
            if not last:
                fwd, state = res[1], res[2]
        send, keep = res[1], res[2]

        mean = reduce_lists(send, keep, True)
        other = swap(mean)
        send, keep = pl.pallas_call(
            functools.partial(margin_kernel, len(sims)),
            out_shape=(f32(TOP, r, LANES),) * 2,
            in_specs=[VMEM] * (len(sims) + 2), out_specs=(VMEM,) * 2,
            scratch_shapes=[
                pltpu.VMEM((targets, LANES), jnp.float32),
                pltpu.VMEM((8, sources), jnp.float32),
                pltpu.VMEM((TOP, targets, LANES), jnp.float32),
                pltpu.VMEM((TOP, sources // LANES, LANES), jnp.float32),
                pltpu.VMEM((TOP, r_targets, LANES), jnp.float32),
            ],
            compiler_params=params(), cost_estimate=cost(30 * sources * targets, 4 * sources * targets),
            name="margin")(*sims, mean, other)
        lists = reduce_lists(send, keep, False)
        other = swap(lists)
        return pl.pallas_call(
            final_kernel, out_shape=(f32(TOP, sources), f32(TOP, targets)),
            in_specs=[VMEM] * 2, out_specs=(VMEM,) * 2, name="final")(lists, other)

    r_targets = 0
    placed = (P("tgt", "src"), P("src"), P("src", "tgt"), P("tgt"))
    return jax.shard_map(
        body, mesh=mesh, in_specs=placed, out_specs=(P(None, "src"), P(None, "tgt")), check_vma=False)
```

```python
import functools
import math

import jax
import jax.numpy as jnp
from jax import lax
from jax.experimental import pallas as pl
from jax.experimental.pallas import tpu as pltpu
from jax.sharding import PartitionSpec as P


TOP = 4
LANES = 128
GROUP = 512
ANY = pl.BlockSpec(memory_space=pl.ANY)
VMEM = pl.BlockSpec(memory_space=pltpu.VMEM)


def params(mib):
    return pltpu.CompilerParams(vmem_limit_bytes=mib << 20)


def exchange(a, b):
    return jnp.maximum(a, b), jnp.minimum(a, b)


def sort4(v):
    a, b, c, d = v
    a, b = exchange(a, b)
    c, d = exchange(c, d)
    a, c = exchange(a, c)
    b, d = exchange(b, d)
    b, c = exchange(b, c)
    return [a, b, c, d]


def merge4(p, q):
    m = [jnp.maximum(p[k], q[TOP - 1 - k]) for k in range(TOP)]
    m[0], m[2] = exchange(m[0], m[2])
    m[1], m[3] = exchange(m[1], m[3])
    m[0], m[1] = exchange(m[0], m[1])
    m[2], m[3] = exchange(m[2], m[3])
    return m


def over_sublanes(lists):
    for shift in (4, 2, 1):
        lists = merge4(lists, [pltpu.roll(x, shift, 0) for x in lists])
    return lists


def sweep_block(load, base, rows, first, lists, state):
    for r in range(0, rows, 32):
        v = [[load(r + 8 * a, b) for b in range(4)] for a in range(4)]
        for b in range(4):
            lists[b] = merge4(lists[b], sort4([v[a][b] for a in range(4)]))
        for a in range(4):
            s = sort4(v[a])
            at = pl.ds(base + (r + 8 * a), 8)
            if not first:
                s = merge4(s, [state[k, at, :] for k in range(TOP)])
            for k in range(TOP):
                state[k, at, :] = s[k]
    return lists


def loop_lists(count, body, write, group):
    def step(q, carried):
        lists = body(q, [list(carried[4 * b : 4 * b + 4]) for b in range(4)])
        return tuple(x for one in lists for x in one)

    empty = tuple(jnp.full((8, LANES), -jnp.inf, jnp.float32) for _ in range(16))
    lists = lax.fori_loop(0, count, step, empty)
    for b in range(4):
        best = over_sublanes(list(lists[4 * b : 4 * b + 4]))
        for k in range(TOP):
            write(k, group * 4 + b, best[k][0:1, :])


def finish_rows(rows, write, state):
    chunks = rows // LANES
    unroll = math.gcd(chunks, 8)

    def one(c):
        x = [state[k, pl.ds(c * LANES, LANES), :].T for k in range(TOP)]
        lists = [[x[k][8 * g : 8 * g + 8, :] for k in range(TOP)] for g in range(LANES // 8)]
        while len(lists) > 1:
            lists = [merge4(lists[i], lists[i + 1]) for i in range(0, len(lists), 2)]
        best = over_sublanes(lists[0])
        for k in range(TOP):
            write(k, c, best[k][0:1, :])

    def body(q, _):
        for h in range(unroll):
            one(q * unroll + h)
        return 0

    lax.fori_loop(0, chunks // unroll, body, 0)


def column_of(row):
    return jnp.broadcast_to(row, (LANES, LANES)).T


def piece_copies(z, core, depth, buf, sem, own, steps):
    copies = []

    def copy(piece, block, place):
        rows = piece.shape[0]
        at = pl.multiple_of((block * 2 + place) * rows, rows)
        return pltpu.make_async_copy(piece, buf.at[pl.ds(at, rows), :], sem.at[len(copies)])

    for place, piece in zip((core, 1 - core), own):
        copies.append((None, copy(piece, z, place)))
    for k, four in steps.items():
        for j in range(2):
            upward = core == j
            block = jnp.where(upward, z - k, z + k)
            valid = jnp.logical_and(block >= 0, block < depth)
            for h in range(2):
                copies.append((valid, copy(four[2 * j + h], block, jnp.where(upward, h, 1 - h))))

    def each(act):
        for valid, c in copies:
            if valid is None:
                act(c)
            else:
                pl.when(valid)(functools.partial(act, c))

    return each


def prep_kernel(masks, depth, steps, first, counts, *refs):
    n, m = counts
    tgt, src = refs[:n], refs[n : n + m]
    if first:
        scale_s, scale_t, tgt_buf, src_buf, column, lane, here_s, here_t, tgt_sem, src_sem, scale_sem = refs[n + m :]
    else:
        _, _, tgt_buf, src_buf, tgt_sem, src_sem = refs[n + m :]
    t, s = lax.axis_index("tgt"), lax.axis_index("src")
    core, z = t % 2, t // 2
    height = tgt[0].shape[0]
    copies = []
    for i in range(n):
        at = jnp.where(core == 0, s ^ masks[i][0], s ^ masks[i][1]) * height
        copies.append(pltpu.make_async_copy(
            tgt[i], tgt_buf.at[pl.ds(pl.multiple_of(at, height), height), :], tgt_sem.at[i]))
    own = 2 if first else 0
    each = piece_copies(z, core, depth, src_buf, src_sem, src[:own],
                        {k: src[own + 4 * i : own + 4 * i + 4] for i, k in enumerate(steps)})
    if first:
        scales = [
            pltpu.make_async_copy(scale_s, here_s, scale_sem.at[0]),
            pltpu.make_async_copy(scale_t, here_t, scale_sem.at[1]),
        ]
        for c in scales:
            c.start()
    for c in copies:
        c.start()
    each(lambda c: c.start())
    if first:
        for c in scales:
            c.wait()
        for c in range(column.shape[0] // LANES):
            column[pl.ds(c * LANES, LANES), :] = column_of(here_t[pl.ds(c, 1), :])
        for c in range(lane.shape[1] // LANES):
            lane[:, pl.ds(c * LANES, LANES)] = jnp.broadcast_to(here_s[pl.ds(c, 1), :], (8, LANES))
    for c in copies:
        c.wait()
    each(lambda c: c.wait())


def score_kernel(depth, *refs):
    late = refs[:4]
    tgt_buf, _, column, lane, src_buf, sim, fwd, bwd, one, two, state, src_sem = refs[4:]
    t = lax.axis_index("tgt")
    core, z = t % 2, t // 2
    sources, targets = src_buf.shape[1], tgt_buf.shape[1]
    each = piece_copies(z, core, depth, src_buf, src_sem, (), {depth - 1: late})
    each(lambda c: c.start())
    each(lambda c: c.wait())
    rows = one.shape[0]
    groups, count = sources // GROUP, targets // rows

    def dot(g, r, out):
        out[...] = lax.dot_general(
            tgt_buf[:, pl.ds(pl.multiple_of(r * rows, rows), rows)],
            src_buf[:, pl.ds(pl.multiple_of(g * GROUP, GROUP), GROUP)],
            (((0,), (0,)), ((), ())), preferred_element_type=jnp.float32)

    def write(k, c, row):
        fwd[k, pl.ds(c, 1), :] = row

    def write_rows(k, c, row):
        bwd[k, pl.ds(c, 1), :] = row

    dot(0, 0, one)
    for g in range(groups):

        def body(q, lists, g=g):
            for h, (now, later) in enumerate(((one, two), (two, one))):
                r = 2 * q + h
                base = pl.multiple_of(r * rows, rows)
                if h == 0:
                    dot(g, r + 1, later)
                else:
                    last = r + 1 == count
                    dot(jnp.where(last, min(g + 1, groups - 1), g), jnp.where(last, 0, r + 1), later)

                def load(row, b, now=now, base=base):
                    cols = pl.ds(g * GROUP + LANES * b, LANES)
                    at = pl.ds(base + row, 8)
                    v = now[row : row + 8, LANES * b : LANES * (b + 1)] * lane[:, cols] * column[at, :]
                    sim[at, cols] = v
                    return v

                lists = sweep_block(load, base, rows, g == 0, lists, state)
            return lists

        loop_lists(count // 2, body, write, g)
    finish_rows(targets, write_rows, state)


def margin_kernel(sim, fwd_mine, fwd_other, bwd_all, fwd, bwd, column, lane, state):
    targets, sources = sim.shape
    f = merge4([fwd_mine[k] for k in range(TOP)], [fwd_other[k] for k in range(TOP)])
    f = 0.5 * (0.25 * (f[0] + f[1] + f[2] + f[3]))
    b = 0.5 * (0.25 * (bwd_all[0] + bwd_all[1] + bwd_all[2] + bwd_all[3]))
    for c in range(targets // LANES):
        column[pl.ds(c * LANES, LANES), :] = column_of(b[c : c + 1, :])
    for c in range(sources // LANES):
        lane[:, pl.ds(c * LANES, LANES)] = jnp.broadcast_to(f[c : c + 1, :], (8, LANES))
    rows = math.gcd(targets, 256)

    def write(k, c, row):
        fwd[k, pl.ds(c, 1), :] = row

    def write_rows(k, c, row):
        bwd[k, pl.ds(c, 1), :] = row

    for g in range(sources // GROUP):

        def body(q, lists, g=g):
            base = pl.multiple_of(q * rows, rows)

            def load(row, b):
                at, cols = pl.ds(base + row, 8), pl.ds(g * GROUP + LANES * b, LANES)
                return sim[at, cols] / (lane[:, cols] + column[at, :])

            return sweep_block(load, base, rows, g == 0, lists, state)

        loop_lists(targets // rows, body, write, g)
    finish_rows(targets, write_rows, state)


def merge_kernel(mine, rec, out):
    merged = merge4([mine[k] for k in range(TOP)], [rec[k] for k in range(TOP)])
    for k in range(TOP):
        out[k] = merged[k]


def final_kernel(fwd_mine, fwd_other, bwd_all, forward, backward):
    f = merge4([fwd_mine[k] for k in range(TOP)], [fwd_other[k] for k in range(TOP)])
    for k in range(TOP):
        for c in range(forward.shape[1] // LANES):
            forward[pl.ds(k, 1), pl.ds(c * LANES, LANES)] = f[k][c : c + 1, :]
        for c in range(backward.shape[1] // LANES):
            backward[pl.ds(k, 1), pl.ds(c * LANES, LANES)] = bwd_all[k, pl.ds(c, 1), :]


def f32(*shape):
    return jax.ShapeDtypeStruct(shape, jnp.float32)


def cost(flops, moved):
    return pl.CostEstimate(flops=flops, bytes_accessed=moved, transcendentals=0)


def solution(mesh):
    n_src, n_tgt = mesh.shape["src"], mesh.shape["tgt"]
    depth = n_tgt // 2
    src_bits, z_bits = n_src.bit_length() - 1, depth.bit_length() - 1
    both = ("src", "tgt")

    def flat(s, t):
        return s * n_tgt + t

    devices = [(s, t) for s in range(n_src) for t in range(n_tgt)]
    partner = [(t, t ^ 1) for t in range(n_tgt)]

    def swap(x):
        return lax.ppermute(x, "tgt", partner)

    def along_z(x, step):
        pairs = []
        for t in range(n_tgt):
            z, core = t // 2, t % 2
            if core == 0 and z >= step - 1 and z + 1 < depth:
                pairs.append((t, t + 2))
            if core == 1 and z <= depth - step and z >= 1:
                pairs.append((t, t - 2))
        return lax.ppermute(x, "tgt", pairs)

    def src_masks(step):
        return 1 << step, 1 << (src_bits - 1 - step)

    def along_src(x, masks):
        pairs = [(flat(s, t), flat(s ^ masks[t % 2], t)) for s, t in devices]
        return lax.ppermute(x, both, pairs)

    def merged(mine, rec):
        return pl.pallas_call(
            merge_kernel, out_shape=f32(*mine.shape), in_specs=[VMEM] * 2, out_specs=VMEM,
            compiler_params=params(1), name="merge")(mine, rec)

    def reduce_lists(fwd, bwd):
        for step in range(max(src_bits, z_bits)):
            if step < z_bits:
                pairs = [(t, t ^ (2 << step)) for t in range(n_tgt)]
                from_z = lax.ppermute(fwd, "tgt", pairs)
            if step < src_bits:
                pairs = [(s, s ^ (1 << step)) for s in range(n_src)]
                from_src = lax.ppermute(bwd, "src", pairs)
            if step < z_bits:
                fwd = merged(fwd, from_z)
            if step < src_bits:
                bwd = merged(bwd, from_src)
        return fwd, swap(fwd), bwd

    def compute(src_codes, src_scale, tgt_codes, tgt_scale):
        sources, targets = src_codes.shape[1], tgt_codes.shape[1]
        total = src_codes.shape[0] * n_tgt
        ns, nt = sources // LANES, targets // LANES
        scale_s, scale_t = src_scale.reshape(-1, LANES), tgt_scale.reshape(-1, LANES)

        u, v = src_codes, swap(src_codes)
        own, passed = [u, v], {}
        for step in range(1, depth):
            u = along_z(u, step)
            v = along_z(v, step)
            passed[step] = [u, v, swap(u), swap(v)]

        held = [(tgt_codes, (0, 0))]
        for step in range(src_bits):
            masks = src_masks(step)
            new = []
            for x, m in held:
                new.append((along_src(x, masks), (m[0] ^ masks[0], m[1] ^ masks[1])))
            held = held + new

        def prep(tgt, steps, extra, first):
            src = (own if first else []) + [x for k in steps for x in passed[k]]
            shapes = [jax.ShapeDtypeStruct((total, targets), tgt_codes.dtype),
                      jax.ShapeDtypeStruct((total, sources), src_codes.dtype)]
            sems = [pltpu.SemaphoreType.DMA((len(tgt),)), pltpu.SemaphoreType.DMA((max(len(src), 1),))]
            if first:
                shapes += [f32(targets, LANES), f32(8, sources)]
                sems = [pltpu.VMEM(scale_s.shape, jnp.float32), pltpu.VMEM(scale_t.shape, jnp.float32)] + sems + [
                    pltpu.SemaphoreType.DMA((2,))]
            count = len(tgt) + len(src)
            return pl.pallas_call(
                functools.partial(prep_kernel, [m for _, m in tgt], depth, steps, first, (len(tgt), len(src))),
                out_shape=shapes, in_specs=[ANY] * count + [ANY if first else VMEM] * 2,
                out_specs=[VMEM] * len(shapes), scratch_shapes=sems,
                input_output_aliases={} if first else {count: 0, count + 1: 1},
                compiler_params=params(2), cost_estimate=cost(0, 4 * total * targets))(*[x for x, _ in tgt], *src, *extra)

        steps = list(range(1, depth - 1))
        tgt_block, src_block, column, lane = prep(held[:1], steps[:-1], (scale_s, scale_t), True)
        tgt_block, src_block = prep(held[1:], steps[-1:], (tgt_block, src_block), False)
        block = min(512, targets // 2)
        _, sim, fwd, bwd = pl.pallas_call(
            functools.partial(score_kernel, depth),
            out_shape=(jax.ShapeDtypeStruct((total, sources), src_codes.dtype),
                       f32(targets, sources), f32(TOP, ns, LANES), f32(TOP, nt, LANES)),
            in_specs=[ANY] * 4 + [VMEM] * 4, out_specs=(VMEM,) * 4,
            input_output_aliases={5: 0},
            scratch_shapes=[
                pltpu.VMEM((block, GROUP), jnp.float32),
                pltpu.VMEM((block, GROUP), jnp.float32),
                pltpu.VMEM((TOP, targets, LANES), jnp.float32),
                pltpu.SemaphoreType.DMA((4,)),
            ],
            compiler_params=params(8), cost_estimate=cost(2 * total * sources * targets, 4 * sources * targets),
            name="score")(*passed[depth - 1], tgt_block, src_block, column, lane)

        fwd, bwd = pl.pallas_call(
            margin_kernel,
            out_shape=(f32(TOP, ns, LANES), f32(TOP, nt, LANES)),
            in_specs=[VMEM] * 4, out_specs=(VMEM,) * 2,
            scratch_shapes=[
                pltpu.VMEM((targets, LANES), jnp.float32),
                pltpu.VMEM((8, sources), jnp.float32),
                pltpu.VMEM((TOP, targets, LANES), jnp.float32),
            ],
            compiler_params=params(8), cost_estimate=cost(30 * sources * targets, 4 * sources * targets),
            name="margin")(sim, *reduce_lists(fwd, bwd))
        return pl.pallas_call(
            final_kernel, out_shape=(f32(TOP, sources), f32(TOP, targets)),
            in_specs=[VMEM] * 3, out_specs=(VMEM,) * 2, compiler_params=params(1),
            name="final")(*reduce_lists(fwd, bwd))

    placed = (P("tgt", "src"), P("src"), P("src", "tgt"), P("tgt"))
    return jax.shard_map(
        compute, mesh=mesh, in_specs=placed, out_specs=(P(None, "src"), P(None, "tgt")), check_vma=False)
```

```python
import functools
import math

import jax
import jax.numpy as jnp
from jax import lax
from jax.experimental import pallas as pl
from jax.experimental.pallas import tpu as pltpu
from jax.sharding import PartitionSpec as P


TOP = 4
LANES = 128
GROUP = 512
ANY = pl.BlockSpec(memory_space=pl.ANY)
VMEM = pl.BlockSpec(memory_space=pltpu.VMEM)


def params(mib):
    return pltpu.CompilerParams(vmem_limit_bytes=mib << 20)


def exchange(a, b):
    return jnp.maximum(a, b), jnp.minimum(a, b)


def sort4(v):
    a, b, c, d = v
    a, b = exchange(a, b)
    c, d = exchange(c, d)
    a, c = exchange(a, c)
    b, d = exchange(b, d)
    b, c = exchange(b, c)
    return [a, b, c, d]


def merge4(p, q):
    m = [jnp.maximum(p[k], q[TOP - 1 - k]) for k in range(TOP)]
    m[0], m[2] = exchange(m[0], m[2])
    m[1], m[3] = exchange(m[1], m[3])
    m[0], m[1] = exchange(m[0], m[1])
    m[2], m[3] = exchange(m[2], m[3])
    return m


def over_sublanes(lists):
    for shift in (4, 2, 1):
        lists = merge4(lists, [pltpu.roll(x, shift, 0) for x in lists])
    return lists


def sweep_block(load, base, rows, first, lists, state):
    for r in range(0, rows, 32):
        v = [[load(r + 8 * a, b) for b in range(4)] for a in range(4)]
        for b in range(4):
            lists[b] = merge4(lists[b], sort4([v[a][b] for a in range(4)]))
        for a in range(4):
            s = sort4(v[a])
            at = pl.ds(base + (r + 8 * a), 8)
            if not first:
                s = merge4(s, [state[k, at, :] for k in range(TOP)])
            for k in range(TOP):
                state[k, at, :] = s[k]
    return lists


def loop_lists(count, body, write, group):
    def step(q, carried):
        lists = body(q, [list(carried[4 * b : 4 * b + 4]) for b in range(4)])
        return tuple(x for one in lists for x in one)

    empty = tuple(jnp.full((8, LANES), -jnp.inf, jnp.float32) for _ in range(16))
    lists = lax.fori_loop(0, count, step, empty)
    for b in range(4):
        best = over_sublanes(list(lists[4 * b : 4 * b + 4]))
        for k in range(TOP):
            write(k, group * 4 + b, best[k][0:1, :])


def finish_rows(rows, write, state):
    chunks = rows // LANES
    unroll = math.gcd(chunks, 8)

    def one(c):
        x = [state[k, pl.ds(c * LANES, LANES), :].T for k in range(TOP)]
        lists = [[x[k][8 * g : 8 * g + 8, :] for k in range(TOP)] for g in range(LANES // 8)]
        while len(lists) > 1:
            lists = [merge4(lists[i], lists[i + 1]) for i in range(0, len(lists), 2)]
        best = over_sublanes(lists[0])
        for k in range(TOP):
            write(k, c, best[k][0:1, :])

    def body(q, _):
        for h in range(unroll):
            one(q * unroll + h)
        return 0

    lax.fori_loop(0, chunks // unroll, body, 0)


def column_of(row):
    return jnp.broadcast_to(row, (LANES, LANES)).T


def piece_copies(z, core, depth, buf, sem, entries):
    copies = []
    for i, (piece, k, j, h, column) in enumerate(entries):
        rows, width = piece.shape
        upward = core == j
        if k == 0:
            block, place, valid = z, jnp.where(upward, 0, 1), None
        else:
            block = jnp.where(upward, z - k, z + k)
            place = jnp.where(upward, h, 1 - h)
            valid = jnp.logical_and(block >= 0, block < depth)
        at = pl.multiple_of((block * 2 + place) * rows, rows)
        copies.append((valid, pltpu.make_async_copy(
            piece, buf.at[pl.ds(at, rows), pl.ds(column, width)], sem.at[i])))

    def each(act):
        for valid, c in copies:
            if valid is None:
                act(c)
            else:
                pl.when(valid)(functools.partial(act, c))

    return each


def prep_kernel(masks, depth, places, first, *refs):
    n, m = len(masks), len(places)
    tgt, src = refs[:n], refs[n : n + m]
    if first:
        scale_s, scale_t, tgt_buf, src_buf, column, lane, here_s, here_t, tgt_sem, src_sem, scale_sem = refs[n + m :]
    else:
        _, _, tgt_buf, src_buf, tgt_sem, src_sem = refs[n + m :]
    t, s = lax.axis_index("tgt"), lax.axis_index("src")
    core, z = t % 2, t // 2
    height = tgt[0].shape[0]
    copies = []
    for i in range(n):
        at = jnp.where(core == 0, s ^ masks[i][0], s ^ masks[i][1]) * height
        copies.append(pltpu.make_async_copy(
            tgt[i], tgt_buf.at[pl.ds(pl.multiple_of(at, height), height), :], tgt_sem.at[i]))
    each = piece_copies(z, core, depth, src_buf, src_sem, [(x, *at) for x, at in zip(src, places)])
    if first:
        scales = [
            pltpu.make_async_copy(scale_s, here_s, scale_sem.at[0]),
            pltpu.make_async_copy(scale_t, here_t, scale_sem.at[1]),
        ]
        for c in scales:
            c.start()
    for c in copies:
        c.start()
    each(lambda c: c.start())
    if first:
        for c in scales:
            c.wait()
        for c in range(column.shape[0] // LANES):
            column[pl.ds(c * LANES, LANES), :] = column_of(here_t[pl.ds(c, 1), :])
        for c in range(lane.shape[1] // LANES):
            lane[:, pl.ds(c * LANES, LANES)] = jnp.broadcast_to(here_s[pl.ds(c, 1), :], (8, LANES))
    for c in copies:
        c.wait()
    each(lambda c: c.wait())


def score_kernel(depth, places, base, last, *refs):
    n = len(places)
    late = refs[:n]
    if last:
        (tgt_buf, _, column, lane, fwd_before, _, src_buf, state, sim, fwd, bwd, one, two, src_sem) = refs[n:]
    else:
        (tgt_buf, _, column, lane, src_buf, state, sim, fwd, one, two, src_sem) = refs[n:]
    t = lax.axis_index("tgt")
    core, z = t % 2, t // 2
    targets = tgt_buf.shape[1]
    each = piece_copies(z, core, depth, src_buf, src_sem, [(x, *at) for x, at in zip(late, places)])
    each(lambda c: c.start())
    each(lambda c: c.wait())
    rows = one.shape[0]
    groups = sim.shape[1] // GROUP
    blocks = [(g, r) for g in range(groups) for r in range(targets // rows)]

    def dot(g, r, out):
        out[...] = lax.dot_general(
            tgt_buf[:, pl.ds(r * rows, rows)], src_buf[:, pl.ds(base + g * GROUP, GROUP)],
            (((0,), (0,)), ((), ())), preferred_element_type=jnp.float32)

    if last:
        before = fwd_before.shape[1]
        fwd[:, :before, :] = fwd_before[...]
    else:
        before = 0

    def write_rows(k, c, row):
        bwd[k, pl.ds(c, 1), :] = row

    dot(*blocks[0], one)
    lists = None
    for i, (g, r) in enumerate(blocks):
        now, later = (one, two) if i % 2 == 0 else (two, one)
        if i + 1 < len(blocks):
            dot(*blocks[i + 1], later)

        def load(row, b, now=now, g=g, r=r):
            at, out = pl.ds(r * rows + row, 8), pl.ds(g * GROUP + LANES * b, LANES)
            v = now[row : row + 8, LANES * b : LANES * (b + 1)]
            v = v * lane[:, pl.ds(base + g * GROUP + LANES * b, LANES)] * column[at, :]
            sim[at, out] = v
            return v

        if r == 0:
            lists = [[jnp.full((8, LANES), -jnp.inf, jnp.float32)] * TOP for _ in range(4)]
        lists = sweep_block(load, r * rows, rows, g == 0 and not last, lists, state)
        if r * rows + rows == targets:
            for b in range(4):
                best = over_sublanes(lists[b])
                for k in range(TOP):
                    fwd[k, pl.ds(before + g * 4 + b, 1), :] = best[k][0:1, :]
    if last:
        finish_rows(targets, write_rows, state)


def margin_kernel(nsim, *refs):
    sims = refs[:nsim]
    fwd_mine, fwd_other, bwd_all, fwd, bwd, column, lane, state = refs[nsim:]
    targets, sources = sims[0].shape[0], sum(x.shape[1] for x in sims)
    f = merge4([fwd_mine[k] for k in range(TOP)], [fwd_other[k] for k in range(TOP)])
    f = 0.5 * (0.25 * (f[0] + f[1] + f[2] + f[3]))
    b = 0.5 * (0.25 * (bwd_all[0] + bwd_all[1] + bwd_all[2] + bwd_all[3]))
    for c in range(targets // LANES):
        column[pl.ds(c * LANES, LANES), :] = column_of(b[c : c + 1, :])
    for c in range(sources // LANES):
        lane[:, pl.ds(c * LANES, LANES)] = jnp.broadcast_to(f[c : c + 1, :], (8, LANES))
    rows = math.gcd(targets, 256)

    def write(k, c, row):
        fwd[k, pl.ds(c, 1), :] = row

    def write_rows(k, c, row):
        bwd[k, pl.ds(c, 1), :] = row

    places = [(x, c) for x in sims for c in range(0, x.shape[1], GROUP)]
    for g, (sim, start) in enumerate(places):

        def body(q, lists, g=g, sim=sim, start=start):
            base = pl.multiple_of(q * rows, rows)

            def load(row, b):
                at, cols = pl.ds(base + row, 8), pl.ds(g * GROUP + LANES * b, LANES)
                return sim[at, pl.ds(start + LANES * b, LANES)] / (lane[:, cols] + column[at, :])

            return sweep_block(load, base, rows, g == 0, lists, state)

        loop_lists(targets // rows, body, write, g)
    finish_rows(targets, write_rows, state)


def merge_kernel(mine, rec, out):
    merged = merge4([mine[k] for k in range(TOP)], [rec[k] for k in range(TOP)])
    for k in range(TOP):
        out[k] = merged[k]


def final_kernel(fwd_mine, fwd_other, bwd_all, forward, backward):
    f = merge4([fwd_mine[k] for k in range(TOP)], [fwd_other[k] for k in range(TOP)])
    for k in range(TOP):
        for c in range(forward.shape[1] // LANES):
            forward[pl.ds(k, 1), pl.ds(c * LANES, LANES)] = f[k][c : c + 1, :]
        for c in range(backward.shape[1] // LANES):
            backward[pl.ds(k, 1), pl.ds(c * LANES, LANES)] = bwd_all[k, pl.ds(c, 1), :]


def in_hbm(x):
    return pltpu.with_memory_space_constraint(x, pltpu.HBM)


def f32(*shape):
    return jax.ShapeDtypeStruct(shape, jnp.float32)


def cost(flops, moved):
    return pl.CostEstimate(flops=flops, bytes_accessed=moved, transcendentals=0)


def solution(mesh):
    n_src, n_tgt = mesh.shape["src"], mesh.shape["tgt"]
    depth = n_tgt // 2
    src_bits, z_bits = n_src.bit_length() - 1, depth.bit_length() - 1
    both = ("src", "tgt")

    def flat(s, t):
        return s * n_tgt + t

    devices = [(s, t) for s in range(n_src) for t in range(n_tgt)]
    partner = [(t, t ^ 1) for t in range(n_tgt)]

    def swap(x):
        return lax.ppermute(x, "tgt", partner)

    def along_z(x, step):
        pairs = []
        for t in range(n_tgt):
            z, core = t // 2, t % 2
            if core == 0 and z >= step - 1 and z + 1 < depth:
                pairs.append((t, t + 2))
            if core == 1 and z <= depth - step and z >= 1:
                pairs.append((t, t - 2))
        return lax.ppermute(x, "tgt", pairs)

    def src_masks(step):
        return 1 << step, 1 << (src_bits - 1 - step)

    def along_src(x, masks):
        pairs = [(flat(s, t), flat(s ^ masks[t % 2], t)) for s, t in devices]
        return lax.ppermute(x, both, pairs)

    def merged(mine, rec):
        return pl.pallas_call(
            merge_kernel, out_shape=f32(*mine.shape), in_specs=[VMEM] * 2, out_specs=VMEM,
            compiler_params=params(1), name="merge")(mine, rec)

    def reduce_lists(fwd, bwd):
        for step in range(max(src_bits, z_bits)):
            if step < z_bits:
                pairs = [(t, t ^ (2 << step)) for t in range(n_tgt)]
                from_z = lax.ppermute(fwd, "tgt", pairs)
            if step < src_bits:
                pairs = [(s, s ^ (1 << step)) for s in range(n_src)]
                from_src = lax.ppermute(bwd, "src", pairs)
            if step < z_bits:
                fwd = merged(fwd, from_z)
            if step < src_bits:
                bwd = merged(bwd, from_src)
        return fwd, swap(fwd), bwd

    def compute(src_codes, src_scale, tgt_codes, tgt_scale):
        sources, targets = src_codes.shape[1], tgt_codes.shape[1]
        total = src_codes.shape[0] * n_tgt
        ns, nt = sources // LANES, targets // LANES
        scale_s, scale_t = src_scale.reshape(-1, LANES), tgt_scale.reshape(-1, LANES)

        u, v = src_codes, swap(src_codes)
        own = [(u, (0, 0, 0, 0)), (v, (0, 1, 0, 0))]
        passed, late = [], []
        for step in range(1, depth):
            u = along_z(u, step)
            pair = [(u, (step, 0, 0, 0)), (swap(u), (step, 1, 0, 0))]
            if step + 1 < depth:
                v = along_z(v, step)
                passed += pair + [(v, (step, 0, 1, 0)), (swap(v), (step, 1, 1, 0))]
            else:
                for start, stop in ((0, GROUP), (GROUP, sources)):
                    part = along_z(v[:, start:stop], step)
                    pair += [(part, (step, 0, 1, start)), (swap(part), (step, 1, 1, start))]
                late = [pair[:4], pair[4:]]

        held = [(tgt_codes, (0, 0))]
        for step in range(src_bits):
            masks = src_masks(step)
            new = []
            for x, m in held:
                new.append((along_src(x, masks), (m[0] ^ masks[0], m[1] ^ masks[1])))
            held = held + new

        def prep(tgt, src, extra, first):
            shapes = [jax.ShapeDtypeStruct((total, targets), tgt_codes.dtype),
                      jax.ShapeDtypeStruct((total, sources), src_codes.dtype)]
            sems = [pltpu.SemaphoreType.DMA((len(tgt),)), pltpu.SemaphoreType.DMA((len(src),))]
            if first:
                shapes += [f32(targets, LANES), f32(8, sources)]
                sems = [pltpu.VMEM(scale_s.shape, jnp.float32), pltpu.VMEM(scale_t.shape, jnp.float32)] + sems + [
                    pltpu.SemaphoreType.DMA((2,))]
            count = len(tgt) + len(src)
            return pl.pallas_call(
                functools.partial(prep_kernel, [m for _, m in tgt], depth, [at for _, at in src], first),
                out_shape=shapes, in_specs=[ANY] * count + [ANY if first else VMEM] * 2,
                out_specs=[VMEM] * len(shapes), scratch_shapes=sems,
                input_output_aliases={} if first else {count: 0, count + 1: 1},
                compiler_params=params(2), cost_estimate=cost(0, 4 * total * targets))(*[x for x, _ in tgt], *[x for x, _ in src], *extra)

        tgt_block, src_block, column, lane = prep(
            [(in_hbm(tgt_codes), (0, 0))], [(in_hbm(src_codes), own[0][1]), own[1]],
            (in_hbm(scale_s), in_hbm(scale_t)), True)
        tgt_block, src_block = prep(held[1:], passed, (tgt_block, src_block), False)

        block = min(512, targets // 2)
        scratch = [pltpu.VMEM((block, GROUP), jnp.float32)] * 2 + [pltpu.SemaphoreType.DMA((4,))]
        buffers = (jax.ShapeDtypeStruct((total, sources), src_codes.dtype), f32(TOP, targets, LANES))

        def score(pieces, base, width, extra, out):
            n, last = len(pieces), bool(extra)
            return pl.pallas_call(
                functools.partial(score_kernel, depth, [at for _, at in pieces], base, last),
                out_shape=buffers + (f32(targets, width),) + out,
                in_specs=[ANY] * n + [VMEM] * (4 + len(extra)), out_specs=(VMEM,) * (3 + len(out)),
                input_output_aliases={n + 1: 0, n + 5: 1} if last else {n + 1: 0},
                scratch_shapes=scratch, compiler_params=params(8),
                cost_estimate=cost(2 * total * width * targets, 4 * width * targets))(
                    *[x for x, _ in pieces], tgt_block, src_block, column, lane, *extra)

        src_block, state, sim_one, fwd = score(
            late[0], 0, GROUP, (), (f32(TOP, GROUP // LANES, LANES),))
        _, _, sim_two, fwd, bwd = score(
            late[1], GROUP, sources - GROUP, (fwd, state), (f32(TOP, ns, LANES), f32(TOP, nt, LANES)))
        sims = (sim_one, sim_two)

        fwd, bwd = pl.pallas_call(
            functools.partial(margin_kernel, len(sims)),
            out_shape=(f32(TOP, ns, LANES), f32(TOP, nt, LANES)),
            in_specs=[VMEM] * (len(sims) + 3), out_specs=(VMEM,) * 2,
            scratch_shapes=[
                pltpu.VMEM((targets, LANES), jnp.float32),
                pltpu.VMEM((8, sources), jnp.float32),
                pltpu.VMEM((TOP, targets, LANES), jnp.float32),
            ],
            compiler_params=params(8), cost_estimate=cost(30 * sources * targets, 4 * sources * targets),
            name="margin")(*sims, *reduce_lists(fwd, bwd))
        return pl.pallas_call(
            final_kernel, out_shape=(f32(TOP, sources), f32(TOP, targets)),
            in_specs=[VMEM] * 3, out_specs=(VMEM,) * 2, compiler_params=params(1),
            name="final")(*reduce_lists(fwd, bwd))

    placed = (P("tgt", "src"), P("src"), P("src", "tgt"), P("tgt"))
    return jax.shard_map(
        compute, mesh=mesh, in_specs=placed, out_specs=(P(None, "src"), P(None, "tgt")), check_vma=False)
```

```python
import functools
import math

import jax
import jax.numpy as jnp
from jax import lax
from jax.experimental import pallas as pl
from jax.experimental.pallas import tpu as pltpu
from jax.sharding import PartitionSpec as P


TOP = 4
LANES = 128
GROUP = 512
ANY = pl.BlockSpec(memory_space=pl.ANY)
VMEM = pl.BlockSpec(memory_space=pltpu.VMEM)


def params(mib):
    return pltpu.CompilerParams(vmem_limit_bytes=mib << 20)


def exchange(a, b):
    return jnp.maximum(a, b), jnp.minimum(a, b)


def sort4(v):
    a, b, c, d = v
    a, b = exchange(a, b)
    c, d = exchange(c, d)
    a, c = exchange(a, c)
    b, d = exchange(b, d)
    b, c = exchange(b, c)
    return [a, b, c, d]


def merge4(p, q):
    m = [jnp.maximum(p[k], q[TOP - 1 - k]) for k in range(TOP)]
    m[0], m[2] = exchange(m[0], m[2])
    m[1], m[3] = exchange(m[1], m[3])
    m[0], m[1] = exchange(m[0], m[1])
    m[2], m[3] = exchange(m[2], m[3])
    return m


def over_sublanes(lists):
    for shift in (4, 2, 1):
        lists = merge4(lists, [pltpu.roll(x, shift, 0) for x in lists])
    return lists


def sweep_block(load, base, rows, first, lists, state):
    for r in range(0, rows, 32):
        v = [[load(r + 8 * a, b) for b in range(4)] for a in range(4)]
        for b in range(4):
            lists[b] = merge4(lists[b], sort4([v[a][b] for a in range(4)]))
        for a in range(4):
            s = sort4(v[a])
            at = pl.ds(base + (r + 8 * a), 8)
            if not first:
                s = merge4(s, [state[k, at, :] for k in range(TOP)])
            for k in range(TOP):
                state[k, at, :] = s[k]
    return lists


def loop_lists(count, body, write, group):
    def step(q, carried):
        lists = body(q, [list(carried[4 * b : 4 * b + 4]) for b in range(4)])
        return tuple(x for one in lists for x in one)

    empty = tuple(jnp.full((8, LANES), -jnp.inf, jnp.float32) for _ in range(16))
    lists = lax.fori_loop(0, count, step, empty)
    for b in range(4):
        best = over_sublanes(list(lists[4 * b : 4 * b + 4]))
        for k in range(TOP):
            write(k, group * 4 + b, best[k][0:1, :])


def finish_rows(rows, write, state):
    chunks = rows // LANES
    unroll = math.gcd(chunks, 8)

    def one(c):
        x = [state[k, pl.ds(c * LANES, LANES), :].T for k in range(TOP)]
        lists = [[x[k][8 * g : 8 * g + 8, :] for k in range(TOP)] for g in range(LANES // 8)]
        while len(lists) > 1:
            lists = [merge4(lists[i], lists[i + 1]) for i in range(0, len(lists), 2)]
        best = over_sublanes(lists[0])
        for k in range(TOP):
            write(k, c, best[k][0:1, :])

    def body(q, _):
        for h in range(unroll):
            one(q * unroll + h)
        return 0

    lax.fori_loop(0, chunks // unroll, body, 0)


def column_of(row):
    return jnp.broadcast_to(row, (LANES, LANES)).T


def piece_copies(z, core, depth, buf, sem, own, steps):
    copies = []

    def copy(piece, block, place):
        rows = piece.shape[0]
        at = pl.multiple_of((block * 2 + place) * rows, rows)
        return pltpu.make_async_copy(piece, buf.at[pl.ds(at, rows), :], sem.at[len(copies)])

    for place, piece in zip((core, 1 - core), own):
        copies.append((None, copy(piece, z, place)))
    for k, four in steps.items():
        for j in range(2):
            upward = core == j
            block = jnp.where(upward, z - k, z + k)
            valid = jnp.logical_and(block >= 0, block < depth)
            for h in range(2):
                copies.append((valid, copy(four[2 * j + h], block, jnp.where(upward, h, 1 - h))))

    def each(act):
        for valid, c in copies:
            if valid is None:
                act(c)
            else:
                pl.when(valid)(functools.partial(act, c))

    return each


def prep_kernel(masks, depth, steps, first, counts, *refs):
    n, m = counts
    tgt, src = refs[:n], refs[n : n + m]
    if first:
        scale_s, scale_t, tgt_buf, src_buf, column, lane, here_s, here_t, tgt_sem, src_sem, scale_sem = refs[n + m :]
    else:
        _, _, tgt_buf, src_buf, tgt_sem, src_sem = refs[n + m :]
    t, s = lax.axis_index("tgt"), lax.axis_index("src")
    core, z = t % 2, t // 2
    height = tgt[0].shape[0]
    copies = []
    for i in range(n):
        at = jnp.where(core == 0, s ^ masks[i][0], s ^ masks[i][1]) * height
        copies.append(pltpu.make_async_copy(
            tgt[i], tgt_buf.at[pl.ds(pl.multiple_of(at, height), height), :], tgt_sem.at[i]))
    own = 2 if first else 0
    each = piece_copies(z, core, depth, src_buf, src_sem, src[:own],
                        {k: src[own + 4 * i : own + 4 * i + 4] for i, k in enumerate(steps)})
    if first:
        scales = [
            pltpu.make_async_copy(scale_s, here_s, scale_sem.at[0]),
            pltpu.make_async_copy(scale_t, here_t, scale_sem.at[1]),
        ]
        for c in scales:
            c.start()
    for c in copies:
        c.start()
    each(lambda c: c.start())
    if first:
        for c in scales:
            c.wait()
        for c in range(column.shape[0] // LANES):
            column[pl.ds(c * LANES, LANES), :] = column_of(here_t[pl.ds(c, 1), :])
        for c in range(lane.shape[1] // LANES):
            lane[:, pl.ds(c * LANES, LANES)] = jnp.broadcast_to(here_s[pl.ds(c, 1), :], (8, LANES))
    for c in copies:
        c.wait()
    each(lambda c: c.wait())


def score_kernel(depth, *refs):
    late = refs[:4]
    tgt_buf, _, column, lane, src_buf, sim, fwd, bwd, one, two, state, src_sem = refs[4:]
    t = lax.axis_index("tgt")
    core, z = t % 2, t // 2
    sources, targets = src_buf.shape[1], tgt_buf.shape[1]
    each = piece_copies(z, core, depth, src_buf, src_sem, (), {depth - 1: late})
    each(lambda c: c.start())
    each(lambda c: c.wait())
    rows = one.shape[0]
    groups, count = sources // GROUP, targets // rows

    def dot(g, r, out):
        out[...] = lax.dot_general(
            tgt_buf[:, pl.ds(pl.multiple_of(r * rows, rows), rows)],
            src_buf[:, pl.ds(pl.multiple_of(g * GROUP, GROUP), GROUP)],
            (((0,), (0,)), ((), ())), preferred_element_type=jnp.float32)

    def write(k, c, row):
        fwd[k, pl.ds(c, 1), :] = row

    def write_rows(k, c, row):
        bwd[k, pl.ds(c, 1), :] = row

    dot(0, 0, one)
    for g in range(groups):

        def body(q, lists, g=g):
            for h, (now, later) in enumerate(((one, two), (two, one))):
                r = 2 * q + h
                base = pl.multiple_of(r * rows, rows)
                if h == 0:
                    dot(g, r + 1, later)
                else:
                    last = r + 1 == count
                    dot(jnp.where(last, min(g + 1, groups - 1), g), jnp.where(last, 0, r + 1), later)

                def load(row, b, now=now, base=base):
                    cols = pl.ds(g * GROUP + LANES * b, LANES)
                    at = pl.ds(base + row, 8)
                    v = now[row : row + 8, LANES * b : LANES * (b + 1)] * lane[:, cols] * column[at, :]
                    sim[at, cols] = v
                    return v

                lists = sweep_block(load, base, rows, g == 0, lists, state)
            return lists

        loop_lists(count // 2, body, write, g)
    finish_rows(targets, write_rows, state)


def margin_kernel(sim, fwd_mine, fwd_other, bwd_all, fwd, bwd, column, lane, state):
    targets, sources = sim.shape
    f = merge4([fwd_mine[k] for k in range(TOP)], [fwd_other[k] for k in range(TOP)])
    f = 0.5 * (0.25 * (f[0] + f[1] + f[2] + f[3]))
    b = 0.5 * (0.25 * (bwd_all[0] + bwd_all[1] + bwd_all[2] + bwd_all[3]))
    for c in range(targets // LANES):
        column[pl.ds(c * LANES, LANES), :] = column_of(b[c : c + 1, :])
    for c in range(sources // LANES):
        lane[:, pl.ds(c * LANES, LANES)] = jnp.broadcast_to(f[c : c + 1, :], (8, LANES))
    rows = math.gcd(targets, 256)

    def write(k, c, row):
        fwd[k, pl.ds(c, 1), :] = row

    def write_rows(k, c, row):
        bwd[k, pl.ds(c, 1), :] = row

    for g in range(sources // GROUP):

        def body(q, lists, g=g):
            base = pl.multiple_of(q * rows, rows)

            def load(row, b):
                at, cols = pl.ds(base + row, 8), pl.ds(g * GROUP + LANES * b, LANES)
                return sim[at, cols] / (lane[:, cols] + column[at, :])

            return sweep_block(load, base, rows, g == 0, lists, state)

        loop_lists(targets // rows, body, write, g)
    finish_rows(targets, write_rows, state)


def merge_kernel(mine, rec, out):
    merged = merge4([mine[k] for k in range(TOP)], [rec[k] for k in range(TOP)])
    for k in range(TOP):
        out[k] = merged[k]


def final_kernel(fwd_mine, fwd_other, bwd_all, forward, backward):
    f = merge4([fwd_mine[k] for k in range(TOP)], [fwd_other[k] for k in range(TOP)])
    for k in range(TOP):
        for c in range(forward.shape[1] // LANES):
            forward[pl.ds(k, 1), pl.ds(c * LANES, LANES)] = f[k][c : c + 1, :]
        for c in range(backward.shape[1] // LANES):
            backward[pl.ds(k, 1), pl.ds(c * LANES, LANES)] = bwd_all[k, pl.ds(c, 1), :]


def in_hbm(x):
    return pltpu.with_memory_space_constraint(x, pltpu.HBM)


def f32(*shape):
    return jax.ShapeDtypeStruct(shape, jnp.float32)


def cost(flops, moved):
    return pl.CostEstimate(flops=flops, bytes_accessed=moved, transcendentals=0)


def solution(mesh):
    n_src, n_tgt = mesh.shape["src"], mesh.shape["tgt"]
    depth = n_tgt // 2
    src_bits, z_bits = n_src.bit_length() - 1, depth.bit_length() - 1
    both = ("src", "tgt")

    def flat(s, t):
        return s * n_tgt + t

    devices = [(s, t) for s in range(n_src) for t in range(n_tgt)]
    partner = [(t, t ^ 1) for t in range(n_tgt)]

    def swap(x):
        return lax.ppermute(x, "tgt", partner)

    def along_z(x, step):
        hop, first = (2, 0) if step == 2 else (1, step - 1)
        pairs = []
        for t in range(n_tgt):
            z, core = t // 2, t % 2
            if core == 0 and z >= first and z + hop < depth:
                pairs.append((t, t + 2 * hop))
            if core == 1 and z < depth - first and z >= hop:
                pairs.append((t, t - 2 * hop))
        return lax.ppermute(x, "tgt", pairs)

    def src_masks(step):
        return 1 << step, 1 << (src_bits - 1 - step)

    def along_src(x, masks):
        pairs = [(flat(s, t), flat(s ^ masks[t % 2], t)) for s, t in devices]
        return lax.ppermute(x, both, pairs)

    def merged(mine, rec):
        return pl.pallas_call(
            merge_kernel, out_shape=f32(*mine.shape), in_specs=[VMEM] * 2, out_specs=VMEM,
            compiler_params=params(1), name="merge")(mine, rec)

    def reduce_lists(fwd, bwd):
        for step in range(max(src_bits, z_bits)):
            if step < z_bits:
                pairs = [(t, t ^ (2 << step)) for t in range(n_tgt)]
                from_z = lax.ppermute(fwd, "tgt", pairs)
            if step < src_bits:
                pairs = [(s, s ^ (1 << step)) for s in range(n_src)]
                from_src = lax.ppermute(bwd, "src", pairs)
            if step < z_bits:
                fwd = merged(fwd, from_z)
            if step < src_bits:
                bwd = merged(bwd, from_src)
        return fwd, swap(fwd), bwd

    def compute(src_codes, src_scale, tgt_codes, tgt_scale):
        sources, targets = src_codes.shape[1], tgt_codes.shape[1]
        total = src_codes.shape[0] * n_tgt
        ns, nt = sources // LANES, targets // LANES
        scale_s, scale_t = src_scale.reshape(-1, LANES), tgt_scale.reshape(-1, LANES)

        u, v = src_codes, swap(src_codes)
        own, passed = [u, v], {}
        for step in range(1, depth):
            u = along_z(own[0] if step == 2 else u, step)
            v = along_z(own[1] if step == 2 else v, step)
            passed[step] = [u, v, swap(u), swap(v)]

        held = [(tgt_codes, (0, 0))]
        for step in range(src_bits):
            masks = src_masks(step)
            new = []
            for x, m in held:
                new.append((along_src(x, masks), (m[0] ^ masks[0], m[1] ^ masks[1])))
            held = held + new

        def prep(tgt, steps, extra, first):
            src = (own if first else []) + [x for k in steps for x in passed[k]]
            if first:
                tgt, src = [(in_hbm(tgt[0][0]), tgt[0][1])], [in_hbm(src[0]), src[1]]
            shapes = [jax.ShapeDtypeStruct((total, targets), tgt_codes.dtype),
                      jax.ShapeDtypeStruct((total, sources), src_codes.dtype)]
            sems = [pltpu.SemaphoreType.DMA((len(tgt),)), pltpu.SemaphoreType.DMA((max(len(src), 1),))]
            if first:
                shapes += [f32(targets, LANES), f32(8, sources)]
                sems = [pltpu.VMEM(scale_s.shape, jnp.float32), pltpu.VMEM(scale_t.shape, jnp.float32)] + sems + [
                    pltpu.SemaphoreType.DMA((2,))]
            count = len(tgt) + len(src)
            return pl.pallas_call(
                functools.partial(prep_kernel, [m for _, m in tgt], depth, steps, first, (len(tgt), len(src))),
                out_shape=shapes, in_specs=[ANY] * count + [ANY if first else VMEM] * 2,
                out_specs=[VMEM] * len(shapes), scratch_shapes=sems,
                input_output_aliases={} if first else {count: 0, count + 1: 1},
                compiler_params=params(2), cost_estimate=cost(0, 4 * total * targets))(*[x for x, _ in tgt], *src, *extra)

        steps = list(range(1, depth - 1))
        tgt_block, src_block, column, lane = prep(held[:1], [], (in_hbm(scale_s), in_hbm(scale_t)), True)
        tgt_block, src_block = prep(held[1:], steps, (tgt_block, src_block), False)
        block = min(512, targets // 2)
        _, sim, fwd, bwd = pl.pallas_call(
            functools.partial(score_kernel, depth),
            out_shape=(jax.ShapeDtypeStruct((total, sources), src_codes.dtype),
                       f32(targets, sources), f32(TOP, ns, LANES), f32(TOP, nt, LANES)),
            in_specs=[ANY] * 4 + [VMEM] * 4, out_specs=(VMEM,) * 4,
            input_output_aliases={5: 0},
            scratch_shapes=[
                pltpu.VMEM((block, GROUP), jnp.float32),
                pltpu.VMEM((block, GROUP), jnp.float32),
                pltpu.VMEM((TOP, targets, LANES), jnp.float32),
                pltpu.SemaphoreType.DMA((4,)),
            ],
            compiler_params=params(8), cost_estimate=cost(2 * total * sources * targets, 4 * sources * targets),
            name="score")(*passed[depth - 1], tgt_block, src_block, column, lane)

        fwd, bwd = pl.pallas_call(
            margin_kernel,
            out_shape=(f32(TOP, ns, LANES), f32(TOP, nt, LANES)),
            in_specs=[VMEM] * 4, out_specs=(VMEM,) * 2,
            scratch_shapes=[
                pltpu.VMEM((targets, LANES), jnp.float32),
                pltpu.VMEM((8, sources), jnp.float32),
                pltpu.VMEM((TOP, targets, LANES), jnp.float32),
            ],
            compiler_params=params(8), cost_estimate=cost(30 * sources * targets, 4 * sources * targets),
            name="margin")(sim, *reduce_lists(fwd, bwd))
        return pl.pallas_call(
            final_kernel, out_shape=(f32(TOP, sources), f32(TOP, targets)),
            in_specs=[VMEM] * 3, out_specs=(VMEM,) * 2, compiler_params=params(1),
            name="final")(*reduce_lists(fwd, bwd))

    placed = (P("tgt", "src"), P("src"), P("src", "tgt"), P("tgt"))
    return jax.shard_map(
        compute, mesh=mesh, in_specs=placed, out_specs=(P(None, "src"), P(None, "tgt")), check_vma=False)
```

```python
import functools
import math

import jax
import jax.numpy as jnp
from jax import lax
from jax.experimental import pallas as pl
from jax.experimental.pallas import tpu as pltpu
from jax.sharding import PartitionSpec as P


TOP = 4
LANES = 128
GROUP = 512
ANY = pl.BlockSpec(memory_space=pl.ANY)
VMEM = pl.BlockSpec(memory_space=pltpu.VMEM)


def params(mib):
    return pltpu.CompilerParams(vmem_limit_bytes=mib << 20)


def exchange(a, b):
    return jnp.maximum(a, b), jnp.minimum(a, b)


def sort4(v):
    a, b, c, d = v
    a, b = exchange(a, b)
    c, d = exchange(c, d)
    a, c = exchange(a, c)
    b, d = exchange(b, d)
    b, c = exchange(b, c)
    return [a, b, c, d]


def merge4(p, q):
    m = [jnp.maximum(p[k], q[TOP - 1 - k]) for k in range(TOP)]
    m[0], m[2] = exchange(m[0], m[2])
    m[1], m[3] = exchange(m[1], m[3])
    m[0], m[1] = exchange(m[0], m[1])
    m[2], m[3] = exchange(m[2], m[3])
    return m


def over_sublanes(lists):
    for shift in (4, 2, 1):
        lists = merge4(lists, [pltpu.roll(x, shift, 0) for x in lists])
    return lists


def sweep_block(load, base, rows, first, lists, state):
    for r in range(0, rows, 32):
        v = [[load(r + 8 * a, b) for b in range(4)] for a in range(4)]
        for b in range(4):
            lists[b] = merge4(lists[b], sort4([v[a][b] for a in range(4)]))
        for a in range(4):
            s = sort4(v[a])
            at = pl.ds(base + (r + 8 * a), 8)
            if not first:
                s = merge4(s, [state[k, at, :] for k in range(TOP)])
            for k in range(TOP):
                state[k, at, :] = s[k]
    return lists


def loop_lists(count, body, write, group):
    def step(q, carried):
        lists = body(q, [list(carried[4 * b : 4 * b + 4]) for b in range(4)])
        return tuple(x for one in lists for x in one)

    empty = tuple(jnp.full((8, LANES), -jnp.inf, jnp.float32) for _ in range(16))
    lists = lax.fori_loop(0, count, step, empty)
    for b in range(4):
        best = over_sublanes(list(lists[4 * b : 4 * b + 4]))
        for k in range(TOP):
            write(k, group * 4 + b, best[k][0:1, :])


def finish_rows(rows, write, state):
    chunks = rows // LANES
    unroll = math.gcd(chunks, 8)

    def one(c):
        x = [state[k, pl.ds(c * LANES, LANES), :].T for k in range(TOP)]
        lists = [[x[k][8 * g : 8 * g + 8, :] for k in range(TOP)] for g in range(LANES // 8)]
        while len(lists) > 1:
            lists = [merge4(lists[i], lists[i + 1]) for i in range(0, len(lists), 2)]
        best = over_sublanes(lists[0])
        for k in range(TOP):
            write(k, c, best[k][0:1, :])

    def body(q, _):
        for h in range(unroll):
            one(q * unroll + h)
        return 0

    lax.fori_loop(0, chunks // unroll, body, 0)


def column_of(row):
    return jnp.broadcast_to(row, (LANES, LANES)).T


def piece_copies(z, core, depth, buf, sem, own, steps):
    copies = []

    def copy(piece, block, place):
        rows = piece.shape[0]
        at = pl.multiple_of((block * 2 + place) * rows, rows)
        return pltpu.make_async_copy(piece, buf.at[pl.ds(at, rows), :], sem.at[len(copies)])

    for place, piece in zip((core, 1 - core), own):
        copies.append((None, copy(piece, z, place)))
    for k, four in steps.items():
        for j in range(2):
            upward = core == j
            block = jnp.where(upward, z - k, z + k)
            valid = jnp.logical_and(block >= 0, block < depth)
            for h in range(2):
                copies.append((valid, copy(four[2 * j + h], block, jnp.where(upward, h, 1 - h))))

    def each(act):
        for valid, c in copies:
            if valid is None:
                act(c)
            else:
                pl.when(valid)(functools.partial(act, c))

    return each


def prep_kernel(masks, depth, steps, first, counts, *refs):
    n, m = counts
    tgt, src = refs[:n], refs[n : n + m]
    if first:
        scale_s, scale_t, tgt_buf, src_buf, column, lane, here_s, here_t, tgt_sem, src_sem, scale_sem = refs[n + m :]
    else:
        _, _, tgt_buf, src_buf, tgt_sem, src_sem = refs[n + m :]
    t, s = lax.axis_index("tgt"), lax.axis_index("src")
    core, z = t % 2, t // 2
    height = tgt[0].shape[0]
    copies = []
    for i in range(n):
        at = jnp.where(core == 0, s ^ masks[i][0], s ^ masks[i][1]) * height
        copies.append(pltpu.make_async_copy(
            tgt[i], tgt_buf.at[pl.ds(pl.multiple_of(at, height), height), :], tgt_sem.at[i]))
    own = 2 if first else 0
    each = piece_copies(z, core, depth, src_buf, src_sem, src[:own],
                        {k: src[own + 4 * i : own + 4 * i + 4] for i, k in enumerate(steps)})
    if first:
        scales = [
            pltpu.make_async_copy(scale_s, here_s, scale_sem.at[0]),
            pltpu.make_async_copy(scale_t, here_t, scale_sem.at[1]),
        ]
        for c in scales:
            c.start()
    for c in copies:
        c.start()
    each(lambda c: c.start())
    if first:
        for c in scales:
            c.wait()
        for c in range(column.shape[0] // LANES):
            column[pl.ds(c * LANES, LANES), :] = column_of(here_t[pl.ds(c, 1), :])
        for c in range(lane.shape[1] // LANES):
            lane[:, pl.ds(c * LANES, LANES)] = jnp.broadcast_to(here_s[pl.ds(c, 1), :], (8, LANES))
    for c in copies:
        c.wait()
    each(lambda c: c.wait())


def score_kernel(depth, *refs):
    late = refs[:4]
    tgt_buf, _, column, lane, src_buf, sim, fwd, bwd, one, two, state, src_sem = refs[4:]
    t = lax.axis_index("tgt")
    core, z = t % 2, t // 2
    sources, targets = src_buf.shape[1], tgt_buf.shape[1]
    each = piece_copies(z, core, depth, src_buf, src_sem, (), {depth - 1: late})
    each(lambda c: c.start())
    each(lambda c: c.wait())
    rows = one.shape[0]
    groups, count = sources // GROUP, targets // rows

    def dot(g, r, out):
        out[...] = lax.dot_general(
            tgt_buf[:, pl.ds(pl.multiple_of(r * rows, rows), rows)],
            src_buf[:, pl.ds(pl.multiple_of(g * GROUP, GROUP), GROUP)],
            (((0,), (0,)), ((), ())), preferred_element_type=jnp.float32)

    def write(k, c, row):
        fwd[k, pl.ds(c, 1), :] = row

    def write_rows(k, c, row):
        bwd[k, pl.ds(c, 1), :] = row

    dot(0, 0, one)
    for g in range(groups):

        def body(q, lists, g=g):
            for h, (now, later) in enumerate(((one, two), (two, one))):
                r = 2 * q + h
                base = pl.multiple_of(r * rows, rows)
                if h == 0:
                    dot(g, r + 1, later)
                else:
                    last = r + 1 == count
                    dot(jnp.where(last, min(g + 1, groups - 1), g), jnp.where(last, 0, r + 1), later)

                def load(row, b, now=now, base=base):
                    cols = pl.ds(g * GROUP + LANES * b, LANES)
                    at = pl.ds(base + row, 8)
                    v = now[row : row + 8, LANES * b : LANES * (b + 1)] * lane[:, cols] * column[at, :]
                    sim[at, cols] = v
                    return v

                lists = sweep_block(load, base, rows, g == 0, lists, state)
            return lists

        loop_lists(count // 2, body, write, g)
    finish_rows(targets, write_rows, state)


def margin_kernel(sim, fwd_mine, fwd_other, bwd_all, fwd, bwd, column, lane, state):
    targets, sources = sim.shape
    f = merge4([fwd_mine[k] for k in range(TOP)], [fwd_other[k] for k in range(TOP)])
    f = 0.5 * (0.25 * (f[0] + f[1] + f[2] + f[3]))
    b = 0.5 * (0.25 * (bwd_all[0] + bwd_all[1] + bwd_all[2] + bwd_all[3]))
    for c in range(targets // LANES):
        column[pl.ds(c * LANES, LANES), :] = column_of(b[c : c + 1, :])
    for c in range(sources // LANES):
        lane[:, pl.ds(c * LANES, LANES)] = jnp.broadcast_to(f[c : c + 1, :], (8, LANES))
    rows = math.gcd(targets, 256)

    def write(k, c, row):
        fwd[k, pl.ds(c, 1), :] = row

    def write_rows(k, c, row):
        bwd[k, pl.ds(c, 1), :] = row

    for g in range(sources // GROUP):

        def body(q, lists, g=g):
            base = pl.multiple_of(q * rows, rows)

            def load(row, b):
                at, cols = pl.ds(base + row, 8), pl.ds(g * GROUP + LANES * b, LANES)
                return sim[at, cols] / (lane[:, cols] + column[at, :])

            return sweep_block(load, base, rows, g == 0, lists, state)

        loop_lists(targets // rows, body, write, g)
    finish_rows(targets, write_rows, state)


def merge_kernel(mine, rec, out):
    merged = merge4([mine[k] for k in range(TOP)], [rec[k] for k in range(TOP)])
    for k in range(TOP):
        out[k] = merged[k]


def final_kernel(fwd_mine, fwd_other, bwd_all, forward, backward):
    f = merge4([fwd_mine[k] for k in range(TOP)], [fwd_other[k] for k in range(TOP)])
    for k in range(TOP):
        for c in range(forward.shape[1] // LANES):
            forward[pl.ds(k, 1), pl.ds(c * LANES, LANES)] = f[k][c : c + 1, :]
        for c in range(backward.shape[1] // LANES):
            backward[pl.ds(k, 1), pl.ds(c * LANES, LANES)] = bwd_all[k, pl.ds(c, 1), :]


def in_hbm(x):
    return pltpu.with_memory_space_constraint(x, pltpu.HBM)


def f32(*shape):
    return jax.ShapeDtypeStruct(shape, jnp.float32)


def cost(flops, moved):
    return pl.CostEstimate(flops=flops, bytes_accessed=moved, transcendentals=0)


def solution(mesh):
    n_src, n_tgt = mesh.shape["src"], mesh.shape["tgt"]
    depth = n_tgt // 2
    src_bits, z_bits = n_src.bit_length() - 1, depth.bit_length() - 1
    both = ("src", "tgt")

    def flat(s, t):
        return s * n_tgt + t

    devices = [(s, t) for s in range(n_src) for t in range(n_tgt)]
    partner = [(t, t ^ 1) for t in range(n_tgt)]

    def swap(x):
        return lax.ppermute(x, "tgt", partner)

    def along_z(x, step):
        pairs = []
        for t in range(n_tgt):
            z, core = t // 2, t % 2
            if core == 0 and z >= step - 1 and z + 1 < depth:
                pairs.append((t, t + 2))
            if core == 1 and z <= depth - step and z >= 1:
                pairs.append((t, t - 2))
        return lax.ppermute(x, "tgt", pairs)

    def src_masks(step):
        return 1 << step, 1 << (src_bits - 1 - step)

    def along_src(x, masks):
        pairs = [(flat(s, t), flat(s ^ masks[t % 2], t)) for s, t in devices]
        return lax.ppermute(x, both, pairs)

    def merged(mine, rec):
        return pl.pallas_call(
            merge_kernel, out_shape=f32(*mine.shape), in_specs=[VMEM] * 2, out_specs=VMEM,
            compiler_params=params(1), name="merge")(mine, rec)

    def reduce_lists(fwd, bwd):
        for step in range(max(src_bits, z_bits)):
            if step < z_bits:
                pairs = [(t, t ^ (2 << step)) for t in range(n_tgt)]
                from_z = lax.ppermute(fwd, "tgt", pairs)
            if step < src_bits:
                pairs = [(s, s ^ (1 << step)) for s in range(n_src)]
                from_src = lax.ppermute(bwd, "src", pairs)
            if step < z_bits:
                fwd = merged(fwd, from_z)
            if step < src_bits:
                bwd = merged(bwd, from_src)
        return fwd, swap(fwd), bwd

    def compute(src_codes, src_scale, tgt_codes, tgt_scale):
        sources, targets = src_codes.shape[1], tgt_codes.shape[1]
        total = src_codes.shape[0] * n_tgt
        ns, nt = sources // LANES, targets // LANES
        scale_s, scale_t = src_scale.reshape(-1, LANES), tgt_scale.reshape(-1, LANES)

        u, v = src_codes, swap(src_codes)
        own, passed = [u, v], {}
        for step in range(1, depth):
            u = along_z(u, step)
            v = along_z(v, step)
            passed[step] = [u, v, swap(u), swap(v)]

        held = [(tgt_codes, (0, 0))]
        for step in range(src_bits):
            masks = src_masks(step)
            new = []
            for x, m in held:
                new.append((along_src(x, masks), (m[0] ^ masks[0], m[1] ^ masks[1])))
            held = held + new

        def prep(tgt, steps, extra, first):
            src = (own if first else []) + [x for k in steps for x in passed[k]]
            if first:
                tgt, src = [(in_hbm(tgt[0][0]), tgt[0][1])], [in_hbm(src[0]), src[1]]
            shapes = [jax.ShapeDtypeStruct((total, targets), tgt_codes.dtype),
                      jax.ShapeDtypeStruct((total, sources), src_codes.dtype)]
            sems = [pltpu.SemaphoreType.DMA((len(tgt),)), pltpu.SemaphoreType.DMA((max(len(src), 1),))]
            if first:
                shapes += [f32(targets, LANES), f32(8, sources)]
                sems = [pltpu.VMEM(scale_s.shape, jnp.float32), pltpu.VMEM(scale_t.shape, jnp.float32)] + sems + [
                    pltpu.SemaphoreType.DMA((2,))]
            count = len(tgt) + len(src)
            return pl.pallas_call(
                functools.partial(prep_kernel, [m for _, m in tgt], depth, steps, first, (len(tgt), len(src))),
                out_shape=shapes, in_specs=[ANY] * count + [ANY if first else VMEM] * 2,
                out_specs=[VMEM] * len(shapes), scratch_shapes=sems,
                input_output_aliases={} if first else {count: 0, count + 1: 1},
                compiler_params=params(2), cost_estimate=cost(0, 4 * total * targets))(*[x for x, _ in tgt], *src, *extra)

        steps = list(range(1, depth - 1))
        tgt_block, src_block, column, lane = prep(held[:1], [], (in_hbm(scale_s), in_hbm(scale_t)), True)
        tgt_block, src_block = prep(held[1:], steps, (tgt_block, src_block), False)
        block = min(512, targets // 2)
        _, sim, fwd, bwd = pl.pallas_call(
            functools.partial(score_kernel, depth),
            out_shape=(jax.ShapeDtypeStruct((total, sources), src_codes.dtype),
                       f32(targets, sources), f32(TOP, ns, LANES), f32(TOP, nt, LANES)),
            in_specs=[ANY] * 4 + [VMEM] * 4, out_specs=(VMEM,) * 4,
            input_output_aliases={5: 0},
            scratch_shapes=[
                pltpu.VMEM((block, GROUP), jnp.float32),
                pltpu.VMEM((block, GROUP), jnp.float32),
                pltpu.VMEM((TOP, targets, LANES), jnp.float32),
                pltpu.SemaphoreType.DMA((4,)),
            ],
            compiler_params=params(8), cost_estimate=cost(2 * total * sources * targets, 4 * sources * targets),
            name="score")(*passed[depth - 1], tgt_block, src_block, column, lane)

        fwd, bwd = pl.pallas_call(
            margin_kernel,
            out_shape=(f32(TOP, ns, LANES), f32(TOP, nt, LANES)),
            in_specs=[VMEM] * 4, out_specs=(VMEM,) * 2,
            scratch_shapes=[
                pltpu.VMEM((targets, LANES), jnp.float32),
                pltpu.VMEM((8, sources), jnp.float32),
                pltpu.VMEM((TOP, targets, LANES), jnp.float32),
            ],
            compiler_params=params(8), cost_estimate=cost(30 * sources * targets, 4 * sources * targets),
            name="margin")(sim, *reduce_lists(fwd, bwd))
        return pl.pallas_call(
            final_kernel, out_shape=(f32(TOP, sources), f32(TOP, targets)),
            in_specs=[VMEM] * 3, out_specs=(VMEM,) * 2, compiler_params=params(1),
            name="final")(*reduce_lists(fwd, bwd))

    placed = (P("tgt", "src"), P("src"), P("src", "tgt"), P("tgt"))
    return jax.shard_map(
        compute, mesh=mesh, in_specs=placed, out_specs=(P(None, "src"), P(None, "tgt")), check_vma=False)
```

```python
import functools
import math

import jax
import jax.numpy as jnp
from jax import lax
from jax.experimental import pallas as pl
from jax.experimental.pallas import tpu as pltpu
from jax.sharding import PartitionSpec as P


TOP = 4
LANES = 128
GROUP = 512
ANY = pl.BlockSpec(memory_space=pl.ANY)
VMEM = pl.BlockSpec(memory_space=pltpu.VMEM)


def params(mib):
    return pltpu.CompilerParams(vmem_limit_bytes=mib << 20)


def exchange(a, b):
    return jnp.maximum(a, b), jnp.minimum(a, b)


def sort4(v):
    a, b, c, d = v
    a, b = exchange(a, b)
    c, d = exchange(c, d)
    a, c = exchange(a, c)
    b, d = exchange(b, d)
    b, c = exchange(b, c)
    return [a, b, c, d]


def merge4(p, q):
    m = [jnp.maximum(p[k], q[TOP - 1 - k]) for k in range(TOP)]
    m[0], m[2] = exchange(m[0], m[2])
    m[1], m[3] = exchange(m[1], m[3])
    m[0], m[1] = exchange(m[0], m[1])
    m[2], m[3] = exchange(m[2], m[3])
    return m


def over_sublanes(lists):
    for shift in (4, 2, 1):
        lists = merge4(lists, [pltpu.roll(x, shift, 0) for x in lists])
    return lists


def sweep_block(load, base, rows, first, lists, state):
    for r in range(0, rows, 32):
        v = [[load(r + 8 * a, b) for b in range(4)] for a in range(4)]
        for b in range(4):
            lists[b] = merge4(lists[b], sort4([v[a][b] for a in range(4)]))
        for a in range(4):
            s = sort4(v[a])
            at = pl.ds(base + (r + 8 * a), 8)
            if not first:
                s = merge4(s, [state[k, at, :] for k in range(TOP)])
            for k in range(TOP):
                state[k, at, :] = s[k]
    return lists


def loop_lists(count, body, write, group):
    def step(q, carried):
        lists = body(q, [list(carried[4 * b : 4 * b + 4]) for b in range(4)])
        return tuple(x for one in lists for x in one)

    empty = tuple(jnp.full((8, LANES), -jnp.inf, jnp.float32) for _ in range(16))
    lists = lax.fori_loop(0, count, step, empty)
    for b in range(4):
        best = over_sublanes(list(lists[4 * b : 4 * b + 4]))
        for k in range(TOP):
            write(k, group * 4 + b, best[k][0:1, :])


def finish_rows(rows, write, state):
    chunks = rows // LANES
    unroll = math.gcd(chunks, 8)

    def one(c):
        x = [state[k, pl.ds(c * LANES, LANES), :].T for k in range(TOP)]
        lists = [[x[k][8 * g : 8 * g + 8, :] for k in range(TOP)] for g in range(LANES // 8)]
        while len(lists) > 1:
            lists = [merge4(lists[i], lists[i + 1]) for i in range(0, len(lists), 2)]
        best = over_sublanes(lists[0])
        for k in range(TOP):
            write(k, c, best[k][0:1, :])

    def body(q, _):
        for h in range(unroll):
            one(q * unroll + h)
        return 0

    lax.fori_loop(0, chunks // unroll, body, 0)


def column_of(row):
    return jnp.broadcast_to(row, (LANES, LANES)).T


def piece_copies(z, core, depth, buf, sem, entries):
    copies = []
    for i, (piece, k, j, h) in enumerate(entries):
        rows = piece.shape[0]
        upward = core == j
        if k == 0:
            block, place, valid = z, jnp.where(upward, 0, 1), None
        else:
            block = jnp.where(upward, z - k, z + k)
            place = jnp.where(upward, h, 1 - h)
            valid = jnp.logical_and(block >= 0, block < depth)
        at = pl.multiple_of((block * 2 + place) * rows, rows)
        copies.append((valid, pltpu.make_async_copy(piece, buf.at[pl.ds(at, rows), :], sem.at[i])))

    def each(act):
        for valid, c in copies:
            if valid is None:
                act(c)
            else:
                pl.when(valid)(functools.partial(act, c))

    return each


def product(targets, sources):
    return lax.dot_general(targets, sources, (((0,), (0,)), ((), ())), preferred_element_type=jnp.float32)


def last_piece(z, core, depth, rows):
    at = pl.multiple_of(jnp.where(z == 0, (depth - 1) * 2 * rows, rows), rows)
    low, high = z == 0, z == depth - 1
    mine = jnp.logical_or(jnp.logical_and(low, core == 1), jnp.logical_and(high, core == 0))
    return at, jnp.logical_or(low, high), mine


def prep_kernel(masks, depth, places, first, *refs):
    n, m = len(masks), len(places)
    tgt, src = refs[:n], refs[n : n + m]
    if first:
        scale_s, scale_t, tgt_buf, src_buf, column, lane, here_s, here_t, tgt_sem, src_sem, scale_sem = refs[n + m :]
    else:
        _, _, tgt_buf, src_buf, part, tgt_sem, src_sem = refs[n + m :]
    t, s = lax.axis_index("tgt"), lax.axis_index("src")
    core, z = t % 2, t // 2
    height = tgt[0].shape[0]
    copies = []
    for i in range(n):
        at = jnp.where(core == 0, s ^ masks[i][0], s ^ masks[i][1]) * height
        copies.append(pltpu.make_async_copy(
            tgt[i], tgt_buf.at[pl.ds(pl.multiple_of(at, height), height), :], tgt_sem.at[i]))
    each = piece_copies(z, core, depth, src_buf, src_sem, [(x, *at) for x, at in zip(src, places)])
    if first:
        scales = [
            pltpu.make_async_copy(scale_s, here_s, scale_sem.at[0]),
            pltpu.make_async_copy(scale_t, here_t, scale_sem.at[1]),
        ]
        for c in scales:
            c.start()
    for c in copies:
        c.start()
    each(lambda c: c.start())
    if first:
        for c in scales:
            c.wait()
        for c in range(column.shape[0] // LANES):
            column[pl.ds(c * LANES, LANES), :] = column_of(here_t[pl.ds(c, 1), :])
        for c in range(lane.shape[1] // LANES):
            lane[:, pl.ds(c * LANES, LANES)] = jnp.broadcast_to(here_s[pl.ds(c, 1), :], (8, LANES))
    for c in copies:
        c.wait()
    each(lambda c: c.wait())
    if not first:
        rows = src[0].shape[0]
        at, missing, _ = last_piece(z, core, depth, rows)

        @pl.when(missing)
        def _():
            src_buf[pl.ds(at, rows), :GROUP] = jnp.zeros((rows, GROUP), src_buf.dtype)

        step = math.gcd(part.shape[0], 256)
        for r in range(0, part.shape[0], step):
            part[pl.ds(r, step), :] = product(tgt_buf[:, pl.ds(r, step)], src_buf[:, :GROUP])


def score_kernel(depth, places, mine_ref, theirs_ref, tgt_buf, _, column, lane, part,
                 src_buf, sim, fwd, bwd, one, two, state, src_sem):
    t = lax.axis_index("tgt")
    core, z = t % 2, t // 2
    sources, targets = src_buf.shape[1], tgt_buf.shape[1]
    each = piece_copies(z, core, depth, src_buf, src_sem,
                        [(x, *at) for x, at in zip((mine_ref, theirs_ref), places)])
    each(lambda c: c.start())
    depth_rows = mine_ref.shape[0]
    slab_at, comes, mine = last_piece(z, core, depth, depth_rows)
    slab = jnp.where(mine, mine_ref[:, :GROUP], theirs_ref[:, :GROUP])
    slab = jnp.where(comes, slab, jnp.zeros_like(slab))
    rows = one.shape[0]
    ns = sources // LANES
    blocks = [(g, r) for g in range(sources // GROUP) for r in range(targets // rows)]

    def dot(g, r, out):
        cols = pl.ds(r * rows, rows)
        if g == 0:
            out[...] = part[cols, :] + product(tgt_buf[pl.ds(slab_at, depth_rows), cols], slab)
        else:
            out[...] = product(tgt_buf[:, cols], src_buf[:, pl.ds(g * GROUP, GROUP)])

    def write_rows(k, c, row):
        bwd[k, pl.ds(c, 1), :] = row

    dot(*blocks[0], one)
    for i, (g, r) in enumerate(blocks):
        now, later = (one, two) if i % 2 == 0 else (two, one)
        if i + 1 < len(blocks):
            if blocks[i + 1] == (1, 0):
                each(lambda c: c.wait())
            dot(*blocks[i + 1], later)

        def load(row, b, now=now, g=g, r=r):
            at, cols = pl.ds(r * rows + row, 8), pl.ds(g * GROUP + LANES * b, LANES)
            v = now[row : row + 8, LANES * b : LANES * (b + 1)] * lane[:, cols] * column[at, :]
            sim[at, cols] = v
            return v

        if r == 0:
            lists = [[jnp.full((8, LANES), -jnp.inf, jnp.float32)] * TOP for _ in range(4)]
        lists = sweep_block(load, r * rows, rows, g == 0, lists, state)
        if r * rows + rows == targets:
            for b in range(4):
                best = over_sublanes(lists[b])
                for k in range(TOP):
                    fwd[pl.ds(k * ns + g * 4 + b, 1), :] = best[k][0:1, :]
    if sources == GROUP:
        each(lambda c: c.wait())
    finish_rows(targets, write_rows, state)


def margin_kernel(sim, fwd_mine, fwd_other, bwd_all, fwd, bwd, column, lane, state):
    targets, sources = sim.shape
    f = merge4(split_list(fwd_mine), split_list(fwd_other))
    f = 0.5 * (0.25 * (f[0] + f[1] + f[2] + f[3]))
    b = 0.5 * (0.25 * (bwd_all[0] + bwd_all[1] + bwd_all[2] + bwd_all[3]))
    for c in range(targets // LANES):
        column[pl.ds(c * LANES, LANES), :] = column_of(b[c : c + 1, :])
    for c in range(sources // LANES):
        lane[:, pl.ds(c * LANES, LANES)] = jnp.broadcast_to(f[c : c + 1, :], (8, LANES))
    rows = math.gcd(targets, 256)

    def write(k, c, row):
        fwd[pl.ds(k * (sources // LANES) + c, 1), :] = row

    def write_rows(k, c, row):
        bwd[k, pl.ds(c, 1), :] = row

    for g in range(sources // GROUP):

        def body(q, lists, g=g):
            base = pl.multiple_of(q * rows, rows)

            def load(row, b):
                at, cols = pl.ds(base + row, 8), pl.ds(g * GROUP + LANES * b, LANES)
                return sim[at, cols] / (lane[:, cols] + column[at, :])

            return sweep_block(load, base, rows, g == 0, lists, state)

        loop_lists(targets // rows, body, write, g)
    finish_rows(targets, write_rows, state)


def split_list(ref):
    n = ref.shape[0] // TOP
    return [ref[n * k : n * (k + 1)] for k in range(TOP)] if len(ref.shape) == 2 else [ref[k] for k in range(TOP)]


def merge_kernel(mine, rec, out):
    merged = merge4(split_list(mine), split_list(rec))
    n = out.shape[0] // TOP
    for k in range(TOP):
        if len(out.shape) == 2:
            out[n * k : n * (k + 1)] = merged[k]
        else:
            out[k] = merged[k]


def final_kernel(fwd_mine, fwd_other, bwd_all, forward, backward):
    f = merge4(split_list(fwd_mine), split_list(fwd_other))
    for k in range(TOP):
        for c in range(forward.shape[1] // LANES):
            forward[pl.ds(k, 1), pl.ds(c * LANES, LANES)] = f[k][c : c + 1, :]
        for c in range(backward.shape[1] // LANES):
            backward[pl.ds(k, 1), pl.ds(c * LANES, LANES)] = bwd_all[k, pl.ds(c, 1), :]


def in_hbm(x):
    return pltpu.with_memory_space_constraint(x, pltpu.HBM)


def f32(*shape):
    return jax.ShapeDtypeStruct(shape, jnp.float32)


def cost(flops, moved):
    return pl.CostEstimate(flops=flops, bytes_accessed=moved, transcendentals=0)


def solution(mesh):
    n_src, n_tgt = mesh.shape["src"], mesh.shape["tgt"]
    depth = n_tgt // 2
    src_bits, z_bits = n_src.bit_length() - 1, depth.bit_length() - 1
    both = ("src", "tgt")

    def flat(s, t):
        return s * n_tgt + t

    devices = [(s, t) for s in range(n_src) for t in range(n_tgt)]
    partner = [(t, t ^ 1) for t in range(n_tgt)]

    def swap(x):
        return lax.ppermute(x, "tgt", partner)

    def along_z(x, step):
        pairs = []
        for t in range(n_tgt):
            z, core = t // 2, t % 2
            if core == 0 and z >= step - 1 and z + 1 < depth:
                pairs.append((t, t + 2))
            if core == 1 and z <= depth - step and z >= 1:
                pairs.append((t, t - 2))
        return lax.ppermute(x, "tgt", pairs)

    def src_masks(step):
        return 1 << step, 1 << (src_bits - 1 - step)

    def along_src(x, masks):
        pairs = [(flat(s, t), flat(s ^ masks[t % 2], t)) for s, t in devices]
        return lax.ppermute(x, both, pairs)

    def merged(mine, rec):
        return pl.pallas_call(
            merge_kernel, out_shape=f32(*mine.shape), in_specs=[VMEM] * 2, out_specs=VMEM,
            compiler_params=params(1), name="merge")(mine, rec)

    def reduce_lists(fwd, bwd):
        for step in range(max(src_bits, z_bits)):
            if step < z_bits:
                pairs = [(t, t ^ (2 << step)) for t in range(n_tgt)]
                from_z = lax.ppermute(fwd, "tgt", pairs)
            if step < src_bits:
                pairs = [(s, s ^ (1 << step)) for s in range(n_src)]
                from_src = lax.ppermute(bwd, "src", pairs)
            if step < z_bits:
                fwd = merged(fwd, from_z)
            if step < src_bits:
                bwd = merged(bwd, from_src)
        return fwd, swap(fwd), bwd

    def compute(src_codes, src_scale, tgt_codes, tgt_scale):
        sources, targets = src_codes.shape[1], tgt_codes.shape[1]
        total = src_codes.shape[0] * n_tgt
        ns, nt = sources // LANES, targets // LANES
        scale_s, scale_t = src_scale.reshape(-1, LANES), tgt_scale.reshape(-1, LANES)

        u, v = src_codes, swap(src_codes)
        own, passed = [(u, (0, 0, 0)), (v, (0, 1, 0))], []
        for step in range(1, depth):
            u = along_z(u, step)
            v = along_z(v, step)
            passed += [(u, (step, 0, 0)), (swap(u), (step, 1, 0)),
                       (v, (step, 0, 1)), (swap(v), (step, 1, 1))]
        passed, late = passed[:-2], passed[-2:]

        held = [(tgt_codes, (0, 0))]
        for step in range(src_bits):
            masks = src_masks(step)
            new = []
            for x, m in held:
                new.append((along_src(x, masks), (m[0] ^ masks[0], m[1] ^ masks[1])))
            held = held + new

        def prep(tgt, src, extra, first):
            shapes = [jax.ShapeDtypeStruct((total, targets), tgt_codes.dtype),
                      jax.ShapeDtypeStruct((total, sources), src_codes.dtype)]
            shapes += [f32(targets, LANES), f32(8, sources)] if first else [f32(targets, GROUP)]
            sems = [pltpu.SemaphoreType.DMA((len(tgt),)), pltpu.SemaphoreType.DMA((len(src),))]
            if first:
                sems = [pltpu.VMEM(scale_s.shape, jnp.float32), pltpu.VMEM(scale_t.shape, jnp.float32)] + sems + [
                    pltpu.SemaphoreType.DMA((2,))]
            count = len(tgt) + len(src)
            return pl.pallas_call(
                functools.partial(prep_kernel, [m for _, m in tgt], depth, [at for _, at in src], first),
                out_shape=shapes, in_specs=[ANY] * count + [ANY if first else VMEM] * 2,
                out_specs=[VMEM] * len(shapes), scratch_shapes=sems,
                input_output_aliases={} if first else {count: 0, count + 1: 1},
                compiler_params=params(4), cost_estimate=cost(0, 4 * total * targets))(*[x for x, _ in tgt], *[x for x, _ in src], *extra)

        tgt_block, src_block, column, lane = prep(
            [(in_hbm(tgt_codes), (0, 0))] + held[1:-1], [(in_hbm(src_codes), own[0][1]), own[1]] + passed[:-6],
            (in_hbm(scale_s), in_hbm(scale_t)), True)
        tgt_block, src_block, part = prep(held[-1:], passed[-6:], (tgt_block, src_block), False)
        block = min(512, targets // 2)
        _, sim, fwd, bwd = pl.pallas_call(
            functools.partial(score_kernel, depth, [at for _, at in late]),
            out_shape=(jax.ShapeDtypeStruct((total, sources), src_codes.dtype),
                       f32(targets, sources), f32(TOP * ns, LANES), f32(TOP, nt, LANES)),
            in_specs=[VMEM] * 7, out_specs=(VMEM,) * 4,
            input_output_aliases={3: 0},
            scratch_shapes=[
                pltpu.VMEM((block, GROUP), jnp.float32),
                pltpu.VMEM((block, GROUP), jnp.float32),
                pltpu.VMEM((TOP, targets, LANES), jnp.float32),
                pltpu.SemaphoreType.DMA((2,)),
            ],
            compiler_params=params(8), cost_estimate=cost(2 * total * sources * targets, 4 * sources * targets),
            name="score")(*[x for x, _ in late], tgt_block, src_block, column, lane, part)

        fwd, bwd = pl.pallas_call(
            margin_kernel,
            out_shape=(f32(TOP * ns, LANES), f32(TOP, nt, LANES)),
            in_specs=[VMEM] * 4, out_specs=(VMEM,) * 2,
            scratch_shapes=[
                pltpu.VMEM((targets, LANES), jnp.float32),
                pltpu.VMEM((8, sources), jnp.float32),
                pltpu.VMEM((TOP, targets, LANES), jnp.float32),
            ],
            compiler_params=params(8), cost_estimate=cost(30 * sources * targets, 4 * sources * targets),
            name="margin")(sim, *reduce_lists(fwd, bwd))
        return pl.pallas_call(
            final_kernel, out_shape=(f32(TOP, sources), f32(TOP, targets)),
            in_specs=[VMEM] * 3, out_specs=(VMEM,) * 2, compiler_params=params(1),
            name="final")(*reduce_lists(fwd, bwd))

    placed = (P("tgt", "src"), P("src"), P("src", "tgt"), P("tgt"))
    return jax.shard_map(
        compute, mesh=mesh, in_specs=placed, out_specs=(P(None, "src"), P(None, "tgt")), check_vma=False)
```

```python
import functools
import math

import jax
import jax.numpy as jnp
from jax import lax
from jax.experimental import pallas as pl
from jax.experimental.pallas import tpu as pltpu
from jax.sharding import PartitionSpec as P


TOP = 4
LANES = 128
GROUP = 512
ANY = pl.BlockSpec(memory_space=pl.ANY)
VMEM = pl.BlockSpec(memory_space=pltpu.VMEM)


def params(mib):
    return pltpu.CompilerParams(vmem_limit_bytes=mib << 20)


def exchange(a, b):
    return jnp.maximum(a, b), jnp.minimum(a, b)


def sort4(v):
    a, b, c, d = v
    a, b = exchange(a, b)
    c, d = exchange(c, d)
    a, c = exchange(a, c)
    b, d = exchange(b, d)
    b, c = exchange(b, c)
    return [a, b, c, d]


def merge4(p, q):
    m = [jnp.maximum(p[k], q[TOP - 1 - k]) for k in range(TOP)]
    m[0], m[2] = exchange(m[0], m[2])
    m[1], m[3] = exchange(m[1], m[3])
    m[0], m[1] = exchange(m[0], m[1])
    m[2], m[3] = exchange(m[2], m[3])
    return m


def over_sublanes(lists):
    for shift in (4, 2, 1):
        lists = merge4(lists, [pltpu.roll(x, shift, 0) for x in lists])
    return lists


def sweep_block(load, base, rows, first, lists, state):
    for r in range(0, rows, 32):
        v = [[load(r + 8 * a, b) for b in range(4)] for a in range(4)]
        for b in range(4):
            lists[b] = merge4(lists[b], sort4([v[a][b] for a in range(4)]))
        for a in range(4):
            s = sort4(v[a])
            at = pl.ds(base + (r + 8 * a), 8)
            if not first:
                s = merge4(s, [state[k, at, :] for k in range(TOP)])
            for k in range(TOP):
                state[k, at, :] = s[k]
    return lists


def loop_lists(count, body, write, group):
    def step(q, carried):
        lists = body(q, [list(carried[4 * b : 4 * b + 4]) for b in range(4)])
        return tuple(x for one in lists for x in one)

    empty = tuple(jnp.full((8, LANES), -jnp.inf, jnp.float32) for _ in range(16))
    lists = lax.fori_loop(0, count, step, empty)
    for b in range(4):
        best = over_sublanes(list(lists[4 * b : 4 * b + 4]))
        for k in range(TOP):
            write(k, group * 4 + b, best[k][0:1, :])


def finish_rows(rows, write, state):
    chunks = rows // LANES
    unroll = math.gcd(chunks, 8)

    def one(c):
        x = [state[k, pl.ds(c * LANES, LANES), :].T for k in range(TOP)]
        lists = [[x[k][8 * g : 8 * g + 8, :] for k in range(TOP)] for g in range(LANES // 8)]
        while len(lists) > 1:
            lists = [merge4(lists[i], lists[i + 1]) for i in range(0, len(lists), 2)]
        best = over_sublanes(lists[0])
        for k in range(TOP):
            write(k, c, best[k][0:1, :])

    def body(q, _):
        for h in range(unroll):
            one(q * unroll + h)
        return 0

    lax.fori_loop(0, chunks // unroll, body, 0)


def column_of(row):
    return jnp.broadcast_to(row, (LANES, LANES)).T


def piece_copies(z, core, depth, buf, sem, entries):
    copies = []
    for i, (piece, k, j, h) in enumerate(entries):
        rows = piece.shape[0]
        upward = core == j
        if k == 0:
            block, place, valid = z, jnp.where(upward, 0, 1), None
        else:
            block = jnp.where(upward, z - k, z + k)
            place = jnp.where(upward, h, 1 - h)
            valid = jnp.logical_and(block >= 0, block < depth)
        at = pl.multiple_of((block * 2 + place) * rows, rows)
        copies.append((valid, pltpu.make_async_copy(piece, buf.at[pl.ds(at, rows), :], sem.at[i])))

    def each(act):
        for valid, c in copies:
            if valid is None:
                act(c)
            else:
                pl.when(valid)(functools.partial(act, c))

    return each


def product(targets, sources):
    return lax.dot_general(targets, sources, (((0,), (0,)), ((), ())), preferred_element_type=jnp.float32)


def last_piece(z, core, depth, rows):
    at = pl.multiple_of(jnp.where(z == 0, (depth - 1) * 2 * rows, rows), rows)
    low, high = z == 0, z == depth - 1
    mine = jnp.logical_or(jnp.logical_and(low, core == 1), jnp.logical_and(high, core == 0))
    return at, jnp.logical_or(low, high), mine


def prep_kernel(masks, depth, places, first, *refs):
    n, m = len(masks), len(places)
    tgt, src = refs[:n], refs[n : n + m]
    if first:
        scale_s, scale_t, tgt_buf, src_buf, column, lane, here_s, here_t, tgt_sem, src_sem, scale_sem = refs[n + m :]
    else:
        _, _, tgt_buf, src_buf, part, tgt_sem, src_sem = refs[n + m :]
    t, s = lax.axis_index("tgt"), lax.axis_index("src")
    core, z = t % 2, t // 2
    height = tgt[0].shape[0]
    copies = []
    for i in range(n):
        at = jnp.where(core == 0, s ^ masks[i][0], s ^ masks[i][1]) * height
        copies.append(pltpu.make_async_copy(
            tgt[i], tgt_buf.at[pl.ds(pl.multiple_of(at, height), height), :], tgt_sem.at[i]))
    each = piece_copies(z, core, depth, src_buf, src_sem, [(x, *at) for x, at in zip(src, places)])
    if first:
        scales = [
            pltpu.make_async_copy(scale_s, here_s, scale_sem.at[0]),
            pltpu.make_async_copy(scale_t, here_t, scale_sem.at[1]),
        ]
        for c in scales:
            c.start()
    for c in copies:
        c.start()
    each(lambda c: c.start())
    if first:
        for c in scales:
            c.wait()
        for c in range(column.shape[0] // LANES):
            column[pl.ds(c * LANES, LANES), :] = column_of(here_t[pl.ds(c, 1), :])
        for c in range(lane.shape[1] // LANES):
            lane[:, pl.ds(c * LANES, LANES)] = jnp.broadcast_to(here_s[pl.ds(c, 1), :], (8, LANES))
    for c in copies:
        c.wait()
    each(lambda c: c.wait())
    if not first:
        rows = src[0].shape[0]
        at, missing, _ = last_piece(z, core, depth, rows)

        @pl.when(missing)
        def _():
            src_buf[pl.ds(at, rows), :GROUP] = jnp.zeros((rows, GROUP), src_buf.dtype)

        step = math.gcd(part.shape[0], 256)
        for r in range(0, part.shape[0], step):
            part[pl.ds(r, step), :] = product(tgt_buf[:, pl.ds(r, step)], src_buf[:, :GROUP])


def score_kernel(depth, places, mine_ref, theirs_ref, tgt_buf, _, column, lane, part,
                 src_buf, sim, fwd, state, one, two, src_sem):
    t = lax.axis_index("tgt")
    core, z = t % 2, t // 2
    sources, targets = src_buf.shape[1], tgt_buf.shape[1]
    each = piece_copies(z, core, depth, src_buf, src_sem,
                        [(x, *at) for x, at in zip((mine_ref, theirs_ref), places)])
    each(lambda c: c.start())
    depth_rows = mine_ref.shape[0]
    slab_at, comes, mine = last_piece(z, core, depth, depth_rows)
    slab = jnp.where(mine, mine_ref[:, :GROUP], theirs_ref[:, :GROUP])
    slab = jnp.where(comes, slab, jnp.zeros_like(slab))
    rows = one.shape[0]
    ns = sources // LANES
    blocks = [(g, r) for g in range(sources // GROUP) for r in range(targets // rows)]

    def dot(g, r, out):
        cols = pl.ds(r * rows, rows)
        if g == 0:
            out[...] = part[cols, :] + product(tgt_buf[pl.ds(slab_at, depth_rows), cols], slab)
        else:
            out[...] = product(tgt_buf[:, cols], src_buf[:, pl.ds(g * GROUP, GROUP)])

    dot(*blocks[0], one)
    for i, (g, r) in enumerate(blocks):
        now, later = (one, two) if i % 2 == 0 else (two, one)
        if i + 1 < len(blocks):
            if blocks[i + 1] == (1, 0):
                each(lambda c: c.wait())
            dot(*blocks[i + 1], later)

        def load(row, b, now=now, g=g, r=r):
            at, cols = pl.ds(r * rows + row, 8), pl.ds(g * GROUP + LANES * b, LANES)
            v = now[row : row + 8, LANES * b : LANES * (b + 1)] * lane[:, cols] * column[at, :]
            sim[at, cols] = v
            return v

        if r == 0:
            lists = [[jnp.full((8, LANES), -jnp.inf, jnp.float32)] * TOP for _ in range(4)]
        lists = sweep_block(load, r * rows, rows, g == 0, lists, state)
        if r * rows + rows == targets:
            for b in range(4):
                best = over_sublanes(lists[b])
                for k in range(TOP):
                    fwd[pl.ds(k * ns + g * 4 + b, 1), :] = best[k][0:1, :]
    if sources == GROUP:
        each(lambda c: c.wait())


def finish_kernel(state, bwd):
    def write(k, c, row):
        bwd[k, pl.ds(c, 1), :] = row

    finish_rows(state.shape[1], write, state)


def column_kernel(mine, rec, column):
    b = merge4(split_list(mine), split_list(rec))
    b = 0.5 * (0.25 * (b[0] + b[1] + b[2] + b[3]))
    for c in range(column.shape[0] // LANES):
        column[pl.ds(c * LANES, LANES), :] = column_of(b[c : c + 1, :])


def margin_kernel(sim, fwd_mine, fwd_other, column, fwd, state, lane):
    targets, sources = sim.shape
    f = merge4(split_list(fwd_mine), split_list(fwd_other))
    f = 0.5 * (0.25 * (f[0] + f[1] + f[2] + f[3]))
    for c in range(sources // LANES):
        lane[:, pl.ds(c * LANES, LANES)] = jnp.broadcast_to(f[c : c + 1, :], (8, LANES))
    rows = math.gcd(targets, 256)

    def write(k, c, row):
        fwd[pl.ds(k * (sources // LANES) + c, 1), :] = row

    for g in range(sources // GROUP):

        def body(q, lists, g=g):
            base = pl.multiple_of(q * rows, rows)

            def load(row, b):
                at, cols = pl.ds(base + row, 8), pl.ds(g * GROUP + LANES * b, LANES)
                return sim[at, cols] / (lane[:, cols] + column[at, :])

            return sweep_block(load, base, rows, g == 0, lists, state)

        loop_lists(targets // rows, body, write, g)


def split_list(ref):
    n = ref.shape[0] // TOP
    return [ref[n * k : n * (k + 1)] for k in range(TOP)] if len(ref.shape) == 2 else [ref[k] for k in range(TOP)]


def merge_kernel(mine, rec, out):
    merged = merge4(split_list(mine), split_list(rec))
    n = out.shape[0] // TOP
    for k in range(TOP):
        if len(out.shape) == 2:
            out[n * k : n * (k + 1)] = merged[k]
        else:
            out[k] = merged[k]


def final_kernel(fwd_mine, fwd_other, bwd_all, forward, backward):
    f = merge4(split_list(fwd_mine), split_list(fwd_other))
    for k in range(TOP):
        for c in range(forward.shape[1] // LANES):
            forward[pl.ds(k, 1), pl.ds(c * LANES, LANES)] = f[k][c : c + 1, :]
        for c in range(backward.shape[1] // LANES):
            backward[pl.ds(k, 1), pl.ds(c * LANES, LANES)] = bwd_all[k, pl.ds(c, 1), :]


def in_hbm(x):
    return pltpu.with_memory_space_constraint(x, pltpu.HBM)


def f32(*shape):
    return jax.ShapeDtypeStruct(shape, jnp.float32)


def cost(flops, moved):
    return pl.CostEstimate(flops=flops, bytes_accessed=moved, transcendentals=0)


def solution(mesh):
    n_src, n_tgt = mesh.shape["src"], mesh.shape["tgt"]
    depth = n_tgt // 2
    src_bits, z_bits = n_src.bit_length() - 1, depth.bit_length() - 1
    both = ("src", "tgt")

    def flat(s, t):
        return s * n_tgt + t

    devices = [(s, t) for s in range(n_src) for t in range(n_tgt)]
    partner = [(t, t ^ 1) for t in range(n_tgt)]

    def swap(x):
        return lax.ppermute(x, "tgt", partner)

    def along_z(x, step):
        pairs = []
        for t in range(n_tgt):
            z, core = t // 2, t % 2
            if core == 0 and z >= step - 1 and z + 1 < depth:
                pairs.append((t, t + 2))
            if core == 1 and z <= depth - step and z >= 1:
                pairs.append((t, t - 2))
        return lax.ppermute(x, "tgt", pairs)

    def src_masks(step):
        return 1 << step, 1 << (src_bits - 1 - step)

    def along_src(x, masks):
        pairs = [(flat(s, t), flat(s ^ masks[t % 2], t)) for s, t in devices]
        return lax.ppermute(x, both, pairs)

    def merged(mine, rec):
        return pl.pallas_call(
            merge_kernel, out_shape=f32(*mine.shape), in_specs=[VMEM] * 2, out_specs=VMEM,
            compiler_params=params(1), name="merge")(mine, rec)

    def reduce_lists(fwd, state, columns):
        targets = state.shape[1]
        for step in range(max(src_bits, z_bits)):
            if step < z_bits:
                pairs = [(t, t ^ (2 << step)) for t in range(n_tgt)]
                from_z = lax.ppermute(fwd, "tgt", pairs)
            if step == 0:
                bwd = pl.pallas_call(
                    finish_kernel, out_shape=f32(TOP, targets // LANES, LANES), in_specs=[VMEM], out_specs=VMEM,
                    compiler_params=params(1), name="finish")(state)
            if step < src_bits:
                pairs = [(s, s ^ (1 << step)) for s in range(n_src)]
                from_src = lax.ppermute(bwd, "src", pairs)
            if step < z_bits:
                fwd = merged(fwd, from_z)
            if step + 1 == src_bits and columns:
                bwd = pl.pallas_call(
                    column_kernel, out_shape=f32(targets, LANES), in_specs=[VMEM] * 2, out_specs=VMEM,
                    compiler_params=params(1), name="column")(bwd, from_src)
            elif step < src_bits:
                bwd = merged(bwd, from_src)
        return fwd, swap(fwd), bwd

    def compute(src_codes, src_scale, tgt_codes, tgt_scale):
        sources, targets = src_codes.shape[1], tgt_codes.shape[1]
        total = src_codes.shape[0] * n_tgt
        ns = sources // LANES
        scale_s, scale_t = src_scale.reshape(-1, LANES), tgt_scale.reshape(-1, LANES)

        u, v = src_codes, swap(src_codes)
        own, passed = [(u, (0, 0, 0)), (v, (0, 1, 0))], []
        for step in range(1, depth):
            u = along_z(u, step)
            v = along_z(v, step)
            passed += [(u, (step, 0, 0)), (swap(u), (step, 1, 0)),
                       (v, (step, 0, 1)), (swap(v), (step, 1, 1))]
        passed, late = passed[:-2], passed[-2:]

        held = [(tgt_codes, (0, 0))]
        for step in range(src_bits):
            masks = src_masks(step)
            new = []
            for x, m in held:
                new.append((along_src(x, masks), (m[0] ^ masks[0], m[1] ^ masks[1])))
            held = held + new

        def prep(tgt, src, extra, first):
            shapes = [jax.ShapeDtypeStruct((total, targets), tgt_codes.dtype),
                      jax.ShapeDtypeStruct((total, sources), src_codes.dtype)]
            shapes += [f32(targets, LANES), f32(8, sources)] if first else [f32(targets, GROUP)]
            sems = [pltpu.SemaphoreType.DMA((len(tgt),)), pltpu.SemaphoreType.DMA((len(src),))]
            if first:
                sems = [pltpu.VMEM(scale_s.shape, jnp.float32), pltpu.VMEM(scale_t.shape, jnp.float32)] + sems + [
                    pltpu.SemaphoreType.DMA((2,))]
            count = len(tgt) + len(src)
            return pl.pallas_call(
                functools.partial(prep_kernel, [m for _, m in tgt], depth, [at for _, at in src], first),
                out_shape=shapes, in_specs=[ANY] * count + [ANY if first else VMEM] * 2,
                out_specs=[VMEM] * len(shapes), scratch_shapes=sems,
                input_output_aliases={} if first else {count: 0, count + 1: 1},
                compiler_params=params(4), cost_estimate=cost(0, 4 * total * targets))(*[x for x, _ in tgt], *[x for x, _ in src], *extra)

        tgt_block, src_block, column, lane = prep(
            [(in_hbm(tgt_codes), (0, 0))] + held[1:-1], [(in_hbm(src_codes), own[0][1]), own[1]] + passed[:-6],
            (in_hbm(scale_s), in_hbm(scale_t)), True)
        tgt_block, src_block, part = prep(held[-1:], passed[-6:], (tgt_block, src_block), False)
        block = min(256, targets // 2)
        _, sim, fwd, state = pl.pallas_call(
            functools.partial(score_kernel, depth, [at for _, at in late]),
            out_shape=(jax.ShapeDtypeStruct((total, sources), src_codes.dtype),
                       f32(targets, sources), f32(TOP * ns, LANES), f32(TOP, targets, LANES)),
            in_specs=[VMEM] * 7, out_specs=(VMEM,) * 4,
            input_output_aliases={3: 0},
            scratch_shapes=[
                pltpu.VMEM((block, GROUP), jnp.float32),
                pltpu.VMEM((block, GROUP), jnp.float32),
                pltpu.SemaphoreType.DMA((2,)),
            ],
            compiler_params=params(8), cost_estimate=cost(2 * total * sources * targets, 4 * sources * targets),
            name="score")(*[x for x, _ in late], tgt_block, src_block, column, lane, part)

        fwd, state = pl.pallas_call(
            margin_kernel,
            out_shape=(f32(TOP * ns, LANES), f32(TOP, targets, LANES)),
            in_specs=[VMEM] * 4, out_specs=(VMEM,) * 2,
            scratch_shapes=[pltpu.VMEM((8, sources), jnp.float32)],
            compiler_params=params(4), cost_estimate=cost(30 * sources * targets, 4 * sources * targets),
            name="margin")(sim, *reduce_lists(fwd, state, True))
        return pl.pallas_call(
            final_kernel, out_shape=(f32(TOP, sources), f32(TOP, targets)),
            in_specs=[VMEM] * 3, out_specs=(VMEM,) * 2, compiler_params=params(1),
            name="final")(*reduce_lists(fwd, state, False))

    placed = (P("tgt", "src"), P("src"), P("src", "tgt"), P("tgt"))
    return jax.shard_map(
        compute, mesh=mesh, in_specs=placed, out_specs=(P(None, "src"), P(None, "tgt")), check_vma=False)
```
